32 devices in a mesh: gx: 8 (over z, x), gy: 4 (over y, core).
Axes of the slice: x: 2, y: 2, z: 4, core: 2. Of those that a mesh axis runs over, the one named last changes fastest.
Arguments:
- field: float32 [20, 64, 64, 256], P(None, 'gx', 'gy'), may hold values from -6 to 6
- spectral_weight: float32 [3, 2, 20, 20, 16, 64, 32], P(None, None, None, None, 'gx', 'gy'), may hold values from -12 to 12
- point_weight: float32 [3, 20, 20], replicated, may hold values from -1.25 to 1.25
- bias: float32 [3, 20], replicated, may hold values from -3 to 3
Outputs:
- result: float32 [20, 64, 64, 256], P(None, 'gx', 'gy')
The draws below stay inside these ranges and needn't reach their ends.
All inputs are finite; a program needn't handle non-finite values.
Results may differ from the reference program's by a relative error of at most 0.00011.
Values sent between devices are 32-bit elements; how exact they have to be, the bound alone decides.
No kernel may reach another device: no remote copies, remote signals or barrier semaphores. Data moves between devices by JAX's collectives and lax.ppermute only.
A program may use at most 192 MiB of HBM per device.

```python
import jax
import jax.numpy as jnp
from jax import lax

C = 20
NZ = 256
MZ = 16
MX = 64
MY = 32
LAYERS = 3
NX = 64
NY = 64


def block_levels(stream_key, dims, shards, least, top_value):
    gain, own = 1.0, jax.random.fold_in(stream_key, 6)
    for position, parts in shards:
        heights = jnp.exp(jax.random.uniform(jax.random.fold_in(own, position), (parts,), jnp.float32, least / len(shards), top_value / len(shards)))
        gain = gain * jnp.repeat(heights, dims[position] // parts).reshape([-1 if axis == position else 1 for axis in range(len(dims))])
    return gain


def centred(key, dims, deviation, limit, split=(), kind=jnp.bfloat16):
    entries = deviation * jax.random.normal(key, dims, jnp.float32)
    if split:
        entries = entries * block_levels(key, dims, split, -0.22, 0.18)
    return jnp.clip(entries, -limit, limit).astype(kind)


def setup_inputs(seed: int = 0) -> dict:
    key_of = jax.random.split(jax.random.key(seed), 5)
    field = centred(key_of[0], (C, NX, NY, NZ), 1.0, 6.0, ((1, 8), (2, 4)), jnp.float32)
    spectral_weight = centred(key_of[1], (LAYERS, 2, C, C, MZ, MX, MY), 2.0, 12.0, ((4, 8), (5, 4)), jnp.float32)
    point_weight = centred(key_of[2], (LAYERS, C, C), C ** -0.5, 1.25, (), jnp.float32)
    bias = centred(key_of[3], (LAYERS, C), 0.5, 3.0, (), jnp.float32)
    return {"field": field, "spectral_weight": spectral_weight, "point_weight": point_weight, "bias": bias}


highest = lax.Precision.HIGHEST


def mode_list(count, points):
    half = count // 2
    lower = jnp.arange(half, dtype=jnp.int32)
    return jnp.concatenate([lower, points - half + lower]).astype(jnp.int32)


def angles(modes, points):
    grid = jnp.arange(points, dtype=jnp.int32)
    product = (grid[:, None] * modes[None, :]) % points
    return (2.0 * jnp.pi / points) * product.astype(jnp.float32)


def forward_table(modes, points):
    phase = angles(modes, points)
    cosine, sine = jnp.cos(phase), jnp.sin(phase)
    return jnp.stack([jnp.stack([cosine, -sine], -1), jnp.stack([sine, cosine], -1)], 1)


def inverse_table(modes, points):
    phase = angles(modes, points).T
    cosine, sine = jnp.cos(phase), jnp.sin(phase)
    return jnp.stack([jnp.stack([cosine, sine], -1), jnp.stack([-sine, cosine], -1)], 0)


def time_tables(total):
    modes = jnp.arange(MZ, dtype=jnp.int32)
    phase = angles(modes, NZ)
    forward = jnp.stack([jnp.cos(phase), -jnp.sin(phase)], -1)
    weight_k = jnp.where(modes == 0, 1.0, 2.0).astype(jnp.float32) / total
    inverse = jnp.stack([jnp.cos(phase).T, -jnp.sin(phase).T], 1) * weight_k[:, None, None]
    return forward, inverse


def mix_modes(spectrum, weights):
    shape = spectrum.shape
    flat = spectrum.reshape(2, shape[1], -1)
    kernel = weights.reshape(2, shape[1], shape[1], -1)

    def paired(left, right):
        return jnp.einsum("cm,com->om", left, right, precision=highest)

    real_part = paired(flat[0], kernel[0]) - paired(flat[1], kernel[1])
    imag_part = paired(flat[0], kernel[1]) + paired(flat[1], kernel[0])
    return jnp.stack([real_part, imag_part]).reshape(shape)


def reference(field, spectral_weight, point_weight, bias):
    kx_modes = mode_list(MX, NX)
    ky_modes = mode_list(MY, NY)
    table_z, inv_z = time_tables(float(NX * NY * NZ))
    table_x = forward_table(kx_modes, NX)
    table_y = forward_table(ky_modes, NY)
    inv_x = inverse_table(kx_modes, NX).transpose(1, 0, 2, 3)
    inv_y = inverse_table(ky_modes, NY)
    current = field
    for layer_index in range(LAYERS):
        spectrum = lax.map(lambda plane: jnp.einsum("xyz,zkp->kpxy", plane, table_z, precision=highest), current)
        spectrum = jnp.einsum("ckpxy,xpjq->ckjqy", spectrum, table_x, precision=highest)
        spectrum = jnp.einsum("ckjpy,ypmq->qckjm", spectrum, table_y, precision=highest)
        mixed = mix_modes(spectrum, spectral_weight[layer_index])
        lines = jnp.einsum("pokjm,pmyq->okjyq", mixed, inv_y, precision=highest)
        planes = jnp.einsum("okjyp,jpxq->okqxy", lines, inv_x, precision=highest)
        previous = current

        def one_channel(packed):
            plane_set, column, shift = packed
            wave = jnp.einsum("kpxy,kpz->xyz", plane_set, inv_z, precision=highest)
            local = jnp.tensordot(column, previous, axes=1, precision=highest)
            return jax.nn.gelu(wave + local + shift, approximate=False)

        current = lax.map(one_channel, (planes, point_weight[layer_index].T, bias[layer_index]))
    return current
```

```python
import functools

import jax
import jax.numpy as jnp
import numpy as np
from jax import lax
from jax.experimental import pallas as pl
from jax.experimental.pallas import tpu as pltpu
from jax.sharding import PartitionSpec as P

MZ = 16
MX = 64
MY = 32
LANES = 128
OCT = 8


def mode_list(count, points):
    half = count // 2
    lower = np.arange(half)
    return np.concatenate([lower, points - half + lower])


def wave_tables(modes, points):
    phase = 2.0 * np.pi / points * ((modes[:, None] * np.arange(points)[None, :]) % points)
    return np.cos(phase), np.sin(phase)


def split(value):
    high = value.astype(jnp.bfloat16)
    low = (value - high.astype(jnp.float32)).astype(jnp.bfloat16)
    return high, low


def outer_split(value):
    high = lax.reduce_precision(value, 8, 7)
    return high.astype(jnp.bfloat16), (value - high).astype(jnp.bfloat16)


def dot3(left, right):
    def one(a, b):
        return jnp.dot(a, b, preferred_element_type=jnp.float32)

    return one(left[0], right[0]) + one(left[1], right[0]) + one(left[0], right[1])


def time_kernel(has_inverse, has_forward, *refs):
    refs = list(refs)
    u_ref = refs.pop(0)
    if has_inverse:
        planes_ref, inv_hi, inv_lo, mix_hi, mix_lo, bias_ref = (refs.pop(0) for _ in range(6))
    if has_forward:
        fwd_hi, fwd_lo = refs.pop(0), refs.pop(0)
    if has_inverse:
        out_ref = refs.pop(0)
    if has_forward:
        spec_ref = refs.pop(0)
    if has_inverse:
        p_hi, p_lo = refs.pop(0), refs.pop(0)
    if has_forward:
        acc = refs.pop(0)
    step = pl.program_id(0)
    channels, _, rows_y, depth = u_ref.shape
    cg = LANES // (2 * rows_y)
    groups = channels // cg

    if has_inverse:

        @pl.when(step == 0)
        def _():
            modes, rows_x, width = planes_ref.shape
            flat = planes_ref[...].reshape(modes * rows_x, width)
            for g in range(groups):
                turned = flat[:, g * LANES : (g + 1) * LANES].T
                high, low = split(turned)
                for c in range(cg):
                    for q in range(2):
                        src = slice((c * 2 + q) * rows_y, (c * 2 + q + 1) * rows_y)
                        dst = slice((g * cg + c) * rows_y, (g * cg + c + 1) * rows_y)
                        n = modes * rows_x
                        p_hi[dst, q * n : (q + 1) * n] = high[src]
                        p_lo[dst, q * n : (q + 1) * n] = low[src]

        wave = dot3((p_hi[...], p_lo[...]), (inv_hi[0], inv_lo[0]))
        wave = wave.reshape(channels, rows_y, depth)
        mixer = (mix_hi[0], mix_lo[0])
        for part in range(rows_y // OCT):
            rows = slice(part * OCT, (part + 1) * OCT)
            x = u_ref[:, 0, rows, :].reshape(channels * OCT, depth)
            local = dot3(mixer, split(x))
            v = wave[:, rows, :].reshape(channels * OCT, depth) + local + bias_ref[0]
            v = v * (lax.erf(v * np.float32(np.sqrt(0.5))) + 1.0) * 0.5
            out_ref[:, 0, rows, :] = v.reshape(channels, OCT, depth)

    if has_forward:
        source = out_ref if has_inverse else u_ref
        g_split = split(source[:, 0, :, :].reshape(channels * rows_y, depth))
        term = dot3(g_split, (fwd_hi[0], fwd_lo[0]))

        @pl.when(step == 0)
        def _():
            acc[...] = term

        @pl.when(step > 0)
        def _():
            acc[...] += term

        @pl.when(step == pl.num_programs(0) - 1)
        def _():
            modes, rows_x, width = spec_ref.shape
            n = modes * rows_x
            for g in range(groups):
                pieces = []
                for c in range(cg):
                    for q in range(2):
                        rows = slice((g * cg + c) * rows_y, (g * cg + c + 1) * rows_y)
                        pieces.append(acc[rows, q * n : (q + 1) * n])
                turned = jnp.concatenate(pieces, axis=0).T
                spec_ref[:, :, g * LANES : (g + 1) * LANES] = turned.reshape(modes, rows_x, LANES)


def time_step(layer, u, planes, tables):
    channels, rows_x, rows_y, depth = u.shape
    has_inverse = planes is not None
    has_forward = tables["fwd"] is not None
    width = channels * 2 * rows_y
    n = MZ * rows_x
    block = pl.BlockSpec((channels, 1, rows_y, depth), lambda s: (0, s, 0, 0))
    args, specs = [u], [block]
    if has_inverse:
        args += [planes, *tables["inv"], *tables["mix"], tables["bias"]]
        specs += [pl.BlockSpec((MZ, rows_x, width), lambda s: (0, 0, 0))]
        specs += [pl.BlockSpec((1, 2 * n, depth), lambda s: (s, 0, 0))] * 2
        side = channels * OCT
        specs += [pl.BlockSpec((1, side, side), lambda s: (layer, 0, 0))] * 2
        specs += [pl.BlockSpec((1, side, depth), lambda s: (layer, 0, 0))]
    if has_forward:
        args += [*tables["fwd"]]
        specs += [pl.BlockSpec((1, depth, 2 * n), lambda s: (s, 0, 0))] * 2
    outs, out_specs, scratch = [], [], []
    if has_inverse:
        outs.append(jax.ShapeDtypeStruct(u.shape, jnp.float32))
        out_specs.append(block)
        scratch += [pltpu.VMEM((channels * rows_y, 2 * n), jnp.bfloat16)] * 2
    if has_forward:
        outs.append(jax.ShapeDtypeStruct((MZ, rows_x, width), jnp.float32))
        out_specs.append(pl.BlockSpec((MZ, rows_x, width), lambda s: (0, 0, 0)))
        scratch += [pltpu.VMEM((channels * rows_y, 2 * n), jnp.float32)]
    return pl.pallas_call(
        functools.partial(time_kernel, has_inverse, has_forward),
        grid=(rows_x,),
        in_specs=specs,
        out_specs=out_specs,
        out_shape=outs,
        scratch_shapes=scratch,
        name="time_step",
    )(*args)


def x_kernel(sign, rows_y, data_ref, t_hi, t_lo, out_ref):
    src, modes_z, per_src, width = data_ref.shape
    dst, _, per_dst, _ = out_ref.shape
    n = dst * per_dst
    lane = lax.broadcasted_iota(jnp.int32, (n, LANES), 1)
    real_lane = (lane // rows_y) % 2 == 0
    for k in range(modes_z):
        d = split(data_ref[:, k].reshape(src * per_src, width))
        both = dot3((t_hi[...], t_lo[...]), d)
        for g in range(width // LANES):
            cols = slice(g * LANES, (g + 1) * LANES)
            cosine, sine = both[:n, cols], both[n:, cols]
            ahead = pltpu.roll(sine, LANES - rows_y, axis=1)
            behind = pltpu.roll(sine, rows_y, axis=1)
            swapped = jnp.where(real_lane, ahead, -behind)
            value = cosine + swapped if sign > 0 else cosine - swapped
            out_ref[:, k, :, cols] = value.reshape(dst, per_dst, LANES)


def x_step(sign, rows_y, data, table, dst):
    src, modes_z, per_src, width = data.shape
    per_dst = table[0].shape[0] // 2 // dst
    return pl.pallas_call(
        functools.partial(x_kernel, sign, rows_y),
        out_shape=jax.ShapeDtypeStruct((dst, modes_z, per_dst, width), jnp.float32),
        name="x_step",
    )(data, *table)


def y_kernel(rows_y, data_ref, w_ref, f_hi, f_lo, i_hi, i_lo, out_ref, left_ref, s_ref, m_ref):
    step = pl.program_id(0)
    count_y, modes_z, local_x, width = data_ref.shape
    groups = width // LANES
    cg = LANES // (2 * rows_y)
    rows = modes_z * local_x
    _, _, channels, per_step, _, _, modes_y = w_ref.shape

    @pl.when(step == 0)
    def _():
        for y in range(count_y):
            block = data_ref[y].reshape(rows, width)
            for g in range(groups):
                left_ref[g * rows : (g + 1) * rows, y * LANES : (y + 1) * LANES] = block[
                    :, g * LANES : (g + 1) * LANES
                ]
        full = dot3(split(left_ref[...]), (f_hi[...], f_lo[...]))
        for g in range(groups):
            for c in range(cg):
                for q in range(2):
                    start = (c * 2 + q) * modes_y
                    s_ref[g * cg + c, q] = full[
                        g * rows : (g + 1) * rows, start : start + modes_y
                    ]

    for o in range(per_step):
        real = jnp.zeros((rows, modes_y), jnp.float32)
        imag = jnp.zeros((rows, modes_y), jnp.float32)
        for c in range(channels):
            wr = w_ref[0, 0, c, o].reshape(rows, modes_y)
            wi = w_ref[0, 1, c, o].reshape(rows, modes_y)
            sr, si = s_ref[c, 0], s_ref[c, 1]
            real += wr * sr - wi * si
            imag += wr * si + wi * sr
        m_ref[step * per_step + o, 0] = real
        m_ref[step * per_step + o, 1] = imag

    @pl.when(step == pl.num_programs(0) - 1)
    def _():
        blocks = []
        for g in range(groups):
            pieces = [m_ref[g * cg + c, q] for c in range(cg) for q in range(2)]
            blocks.append(jnp.concatenate(pieces, axis=1))
        lines = dot3(split(jnp.concatenate(blocks, axis=0)), (i_hi[...], i_lo[...]))
        for y in range(count_y):
            for g in range(groups):
                piece = lines[g * rows : (g + 1) * rows, y * LANES : (y + 1) * LANES]
                out_ref[y, :, :, g * LANES : (g + 1) * LANES] = piece.reshape(
                    modes_z, local_x, LANES
                )


def y_step(layer, rows_y, data, weights, forward, inverse):
    count_y, modes_z, local_x, width = data.shape
    _, _, channels, _, _, _, modes_y = weights.shape
    per_step = 4 if channels % 4 == 0 else 1
    rows = modes_z * local_x
    groups = width // LANES
    cg = LANES // (2 * rows_y)
    whole = lambda s: (0, 0)
    return pl.pallas_call(
        functools.partial(y_kernel, rows_y),
        grid=(channels // per_step,),
        in_specs=[
            pl.BlockSpec(data.shape, lambda s: (0, 0, 0, 0)),
            pl.BlockSpec(
                (1, 2, channels, per_step, modes_z, local_x, modes_y),
                lambda s: (layer, 0, 0, s, 0, 0, 0),
            ),
            pl.BlockSpec(forward[0].shape, whole),
            pl.BlockSpec(forward[1].shape, whole),
            pl.BlockSpec(inverse[0].shape, whole),
            pl.BlockSpec(inverse[1].shape, whole),
        ],
        out_specs=pl.BlockSpec(data.shape, lambda s: (0, 0, 0, 0)),
        out_shape=jax.ShapeDtypeStruct(data.shape, jnp.float32),
        scratch_shapes=[
            pltpu.VMEM((groups * rows, count_y * LANES), jnp.float32),
            pltpu.VMEM((channels, 2, rows, modes_y), jnp.float32),
            pltpu.VMEM((channels, 2, rows, modes_y), jnp.float32),
        ],
        name="y_step",
    )(data, weights, *forward, *inverse)


def time_table(rows_x, depth, total):
    cosine, sine = wave_tables(np.arange(MZ), depth)
    weight = np.where(np.arange(MZ) == 0, 1.0, 2.0)[:, None] / total
    fwd = jnp.asarray(np.stack([cosine, -sine]), jnp.float32)
    inv = jnp.asarray(np.stack([cosine * weight, -sine * weight]), jnp.float32)
    n = 2 * MZ * rows_x
    row = lax.broadcasted_iota(jnp.int32, (rows_x, n, depth), 0)
    col = lax.broadcasted_iota(jnp.int32, (rows_x, n, depth), 1) % rows_x
    wide = jnp.repeat(inv.reshape(2 * MZ, depth), rows_x, axis=0)[None]
    inverse = jnp.where(row == col, wide, 0.0)
    row = lax.broadcasted_iota(jnp.int32, (rows_x, depth, n), 0)
    col = lax.broadcasted_iota(jnp.int32, (rows_x, depth, n), 2) % rows_x
    wide = jnp.repeat(fwd.reshape(2 * MZ, depth).T, rows_x, axis=1)[None]
    forward = jnp.where(row == col, wide, 0.0)
    return outer_split(forward), outer_split(inverse)


def constant_split(table):
    high = np.asarray(table, np.float32).astype(jnp.bfloat16)
    low = (np.asarray(table, np.float32) - high.astype(np.float32)).astype(jnp.bfloat16)
    return jnp.asarray(high), jnp.asarray(low)


def y_tables(points_y, rows_y):
    cosine, sine = wave_tables(mode_list(MY, points_y), points_y)
    count = points_y // rows_y
    cg = LANES // (2 * rows_y)
    cosine = cosine.reshape(MY, count, rows_y)
    sine = sine.reshape(MY, count, rows_y)
    fwd = np.stack([np.stack([cosine, -sine]), np.stack([sine, cosine])])
    inv = np.stack([np.stack([cosine, sine]), np.stack([-sine, cosine])])
    eye = np.eye(cg)
    fwd = np.einsum("ab,rqmgy->garybqm", eye, fwd).reshape(count * LANES, cg * 2 * MY)
    inv = np.einsum("ab,qrmgy->aqmgbry", eye, inv).reshape(cg * 2 * MY, count * LANES)
    return constant_split(fwd), constant_split(inv)


def shards(field, spectral_weight, point_weight, bias):
    channels, rows_x, rows_y, depth = field.shape
    layers = spectral_weight.shape[0]
    count_x = lax.axis_size("gx")
    count_y = lax.axis_size("gy")
    points_x = rows_x * count_x
    points_y = rows_y * count_y
    local_z = MZ // count_x
    local_x = MX // count_y
    fwd_z, inv_z = time_table(rows_x, depth, float(points_x * points_y * depth))
    cosine, sine = wave_tables(mode_list(MX, points_x), points_x)
    fwd_x = constant_split(np.concatenate([cosine, sine], 0))
    inv_x = constant_split(np.concatenate([cosine.T, sine.T], 0))
    fwd_y, inv_y = y_tables(points_y, rows_y)
    eye = jnp.eye(OCT, dtype=jnp.float32)
    mixer = jnp.einsum("lco,yv->loycv", point_weight, eye, precision=lax.Precision.HIGHEST)
    mixer = outer_split(mixer.reshape(layers, channels * OCT, channels * OCT))
    wide_bias = jnp.broadcast_to(
        jnp.repeat(bias, OCT, axis=1)[:, :, None], (layers, channels * OCT, depth)
    )
    tables = {"fwd": fwd_z, "inv": inv_z, "mix": mixer, "bias": wide_bias}
    last = dict(tables, fwd=None)

    current = field
    (spectrum,) = time_step(0, current, None, tables)
    for layer in range(layers):
        data = spectrum.reshape(count_x, local_z, rows_x, -1)
        data = lax.all_to_all(data, "gx", 0, 0)
        data = x_step(1, rows_y, data, fwd_x, count_y)
        data = lax.all_to_all(data, "gy", 0, 0)
        data = y_step(layer, rows_y, data, spectral_weight, fwd_y, inv_y)
        data = lax.all_to_all(data, "gy", 0, 0)
        data = x_step(-1, rows_y, data, inv_x, count_x)
        data = lax.all_to_all(data, "gx", 0, 0)
        planes = data.reshape(MZ, rows_x, -1)
        if layer + 1 < layers:
            current, spectrum = time_step(layer, current, planes, tables)
        else:
            (current,) = time_step(layer, current, planes, last)
    return current


def solution(mesh):
    return jax.shard_map(
        shards,
        mesh=mesh,
        in_specs=(P(None, "gx", "gy", None), P(None, None, None, None, "gx", "gy", None), P(), P()),
        out_specs=P(None, "gx", "gy", None),
        check_vma=False,
    )
```

```python
import functools

import jax
import jax.numpy as jnp
import numpy as np
from jax import lax
from jax.experimental import pallas as pl
from jax.experimental.pallas import tpu as pltpu
from jax.sharding import PartitionSpec as P

MZ = 16
MX = 64
MY = 32
LANES = 128
OCT = 8


def mode_list(count, points):
    half = count // 2
    lower = np.arange(half)
    return np.concatenate([lower, points - half + lower])


def wave_tables(modes, points):
    phase = 2.0 * np.pi / points * ((modes[:, None] * np.arange(points)[None, :]) % points)
    return np.cos(phase), np.sin(phase)


def split(value):
    high = value.astype(jnp.bfloat16)
    low = (value - high.astype(jnp.float32)).astype(jnp.bfloat16)
    return high, low


def dot3(left, right):
    def one(a, b):
        return jnp.dot(a, b, preferred_element_type=jnp.float32)

    return one(left[0], right[0]) + one(left[1], right[0]) + one(left[0], right[1])


def time_kernel(layer, has_inverse, has_forward, *refs):
    refs = list(refs)
    u_ref = refs.pop(0)
    if has_inverse:
        planes_ref, inv_hi, inv_lo, point_ref, bias_ref = (refs.pop(0) for _ in range(5))
    if has_forward:
        fwd_hi, fwd_lo = refs.pop(0), refs.pop(0)
    if has_inverse:
        out_ref = refs.pop(0)
    if has_forward:
        spec_ref = refs.pop(0)
    if has_inverse:
        p_hi, p_lo, mix_hi, mix_lo, wide_bias = (refs.pop(0) for _ in range(5))
    if has_forward:
        acc = refs.pop(0)
    step = pl.program_id(0)
    rows_x = pl.num_programs(0)
    channels, _, rows_y, depth = u_ref.shape
    cg = LANES // (2 * rows_y)
    groups = channels // cg

    if has_inverse:

        @pl.when(step == 0)
        def _():
            modes, local, width = planes_ref.shape
            n = modes * local
            flat = planes_ref[...].reshape(n, width)
            for g in range(groups):
                turned = flat[:, g * LANES : (g + 1) * LANES].T
                high, low = split(turned)
                for c in range(cg):
                    for q in range(2):
                        src = slice((c * 2 + q) * rows_y, (c * 2 + q + 1) * rows_y)
                        dst = slice((g * cg + c) * rows_y, (g * cg + c + 1) * rows_y)
                        p_hi[dst, q * n : (q + 1) * n] = high[src]
                        p_lo[dst, q * n : (q + 1) * n] = low[src]
            side = channels * OCT
            pick = lax.broadcasted_iota(jnp.int32, (side, channels), 0) // OCT
            pick = (pick == lax.broadcasted_iota(jnp.int32, (side, channels), 1)).astype(
                jnp.bfloat16
            )
            place = lax.broadcasted_iota(jnp.int32, (channels, side), 1) // OCT
            place = (place == lax.broadcasted_iota(jnp.int32, (channels, side), 0)).astype(
                jnp.bfloat16
            )
            same = lax.broadcasted_iota(jnp.int32, (side, side), 0) % OCT
            same = same == lax.broadcasted_iota(jnp.int32, (side, side), 1) % OCT
            contract = (((1,), (1,)), ((), ()))
            for part, target in zip(split(point_ref[layer]), (mix_hi, mix_lo)):
                rows = lax.dot_general(pick, part, contract, preferred_element_type=jnp.float32)
                full = jnp.dot(
                    rows.astype(jnp.bfloat16), place, preferred_element_type=jnp.float32
                )
                target[...] = jnp.where(same, full, 0.0).astype(jnp.bfloat16)
            lines = jnp.broadcast_to(bias_ref[layer : layer + 1, :], (LANES, channels))
            first = lines.astype(jnp.bfloat16)
            rest = lines - first.astype(jnp.float32)
            second, third = split(rest)
            wide_bias[...] = sum(
                lax.dot_general(pick, part, contract, preferred_element_type=jnp.float32)
                for part in (third, second, first)
            )

        n2 = p_hi.shape[1]
        lane = lax.broadcasted_iota(jnp.int32, (OCT, n2), 1)
        keep = jnp.where(lane % rows_x == step, 1.0, 0.0).astype(jnp.bfloat16)[0:1]
        wave = dot3((p_hi[...] * keep, p_lo[...] * keep), (inv_hi[...], inv_lo[...]))
        wave = wave.reshape(channels, rows_y, depth)
        mixer = (mix_hi[...], mix_lo[...])
        shift = jnp.concatenate([wide_bias[...]] * (depth // LANES), axis=1)
        for part in range(rows_y // OCT):
            rows = slice(part * OCT, (part + 1) * OCT)
            x = u_ref[:, 0, rows, :].reshape(channels * OCT, depth)
            local = dot3(mixer, split(x))
            v = wave[:, rows, :].reshape(channels * OCT, depth) + local + shift
            v = v * (lax.erf(v * np.float32(np.sqrt(0.5))) + 1.0) * 0.5
            out_ref[:, 0, rows, :] = v.reshape(channels, OCT, depth)

    if has_forward:
        source = out_ref if has_inverse else u_ref
        g_split = split(source[:, 0, :, :].reshape(channels * rows_y, depth))
        term = dot3(g_split, (fwd_hi[...], fwd_lo[...]))

        @pl.when(step == 0)
        def _():
            acc[...] = term

        @pl.when(step > 0)
        def _():
            lane = lax.broadcasted_iota(jnp.int32, term.shape, 1)
            acc[...] = jnp.where(lane % rows_x == step, term, acc[...])

        @pl.when(step == rows_x - 1)
        def _():
            modes, local, width = spec_ref.shape
            n = modes * local
            for g in range(groups):
                pieces = []
                for c in range(cg):
                    for q in range(2):
                        rows = slice((g * cg + c) * rows_y, (g * cg + c + 1) * rows_y)
                        pieces.append(acc[rows, q * n : (q + 1) * n])
                turned = jnp.concatenate(pieces, axis=0).T
                spec_ref[:, :, g * LANES : (g + 1) * LANES] = turned.reshape(modes, local, LANES)


def time_step(layer, u, planes, tables, point_weight, bias):
    channels, rows_x, rows_y, depth = u.shape
    has_inverse = planes is not None
    has_forward = tables["fwd"] is not None
    width = channels * 2 * rows_y
    n = MZ * rows_x
    side = channels * OCT
    block = pl.BlockSpec((channels, 1, rows_y, depth), lambda s: (0, s, 0, 0))

    def whole(shape):
        return pl.BlockSpec(shape, lambda s: (0,) * len(shape))

    args, specs = [u], [block]
    if has_inverse:
        rest = [planes, *tables["inv"], point_weight, bias]
        args += rest
        specs += [whole(a.shape) for a in rest]
    if has_forward:
        args += [*tables["fwd"]]
        specs += [whole(a.shape) for a in tables["fwd"]]
    outs, out_specs, scratch = [], [], []
    if has_inverse:
        outs.append(jax.ShapeDtypeStruct(u.shape, jnp.float32))
        out_specs.append(block)
        scratch += [pltpu.VMEM((channels * rows_y, 2 * n), jnp.bfloat16)] * 2
        scratch += [pltpu.VMEM((side, side), jnp.bfloat16)] * 2
        scratch += [pltpu.VMEM((side, LANES), jnp.float32)]
    if has_forward:
        outs.append(jax.ShapeDtypeStruct((MZ, rows_x, width), jnp.float32))
        out_specs.append(whole((MZ, rows_x, width)))
        scratch += [pltpu.VMEM((channels * rows_y, 2 * n), jnp.float32)]
    return pl.pallas_call(
        functools.partial(time_kernel, layer, has_inverse, has_forward),
        grid=(rows_x,),
        in_specs=specs,
        out_specs=out_specs,
        out_shape=outs,
        scratch_shapes=scratch,
        compiler_params=pltpu.CompilerParams(vmem_limit_bytes=14 << 20),
        name="time_step",
    )(*args)


def turn(sign, rows_y, cosine, sine):
    lane = lax.broadcasted_iota(jnp.int32, cosine.shape, 1)
    ahead = pltpu.roll(sine, LANES - rows_y, axis=1)
    behind = pltpu.roll(sine, rows_y, axis=1)
    swapped = jnp.where((lane // rows_y) % 2 == 0, ahead, -behind)
    return cosine + swapped if sign > 0 else cosine - swapped


def x_forward_kernel(rows_y, data_ref, t_hi, t_lo, *out_refs):
    me = lax.axis_index("gy")
    src, modes_z, per_src, width = data_ref.shape
    _, per_dst, _ = out_refs[0].shape
    table = [
        jnp.concatenate([t[jnp.bitwise_xor(me, s)] for s in range(len(out_refs))], axis=0)
        for t in (t_hi, t_lo)
    ]
    for k in range(modes_z):
        both = dot3(table, split(data_ref[:, k].reshape(src * per_src, width)))
        for s, out_ref in enumerate(out_refs):
            top = 2 * s * per_dst
            for g in range(width // LANES):
                cols = slice(g * LANES, (g + 1) * LANES)
                cosine = both[top : top + per_dst, cols]
                sine = both[top + per_dst : top + 2 * per_dst, cols]
                out_ref[k, :, cols] = turn(1, rows_y, cosine, sine)


def x_forward(rows_y, data, table):
    src, modes_z, per_src, width = data.shape
    count_y, twice, _ = table[0].shape
    return pl.pallas_call(
        functools.partial(x_forward_kernel, rows_y),
        out_shape=[jax.ShapeDtypeStruct((modes_z, twice // 2, width), jnp.float32)] * count_y,
        compiler_params=pltpu.CompilerParams(vmem_limit_bytes=8 << 20),
        name="x_forward",
    )(data, *table)


def x_inverse_kernel(rows_y, *refs):
    *data_refs, t_hi, t_lo, out_ref, work = refs
    me = lax.axis_index("gy")
    for s, data_ref in enumerate(data_refs):
        work[jnp.bitwise_xor(me, s)] = data_ref[...]
    src, modes_z, per_src, width = work.shape
    dst, _, per_dst, _ = out_ref.shape
    n = dst * per_dst
    table = (t_hi[...], t_lo[...])
    for k in range(modes_z):
        both = dot3(table, split(work[:, k].reshape(src * per_src, width)))
        for g in range(width // LANES):
            cols = slice(g * LANES, (g + 1) * LANES)
            value = turn(-1, rows_y, both[:n, cols], both[n:, cols])
            out_ref[:, k, :, cols] = value.reshape(dst, per_dst, LANES)


def x_inverse(rows_y, parts, table, dst):
    modes_z, per_src, width = parts[0].shape
    per_dst = table[0].shape[0] // 2 // dst
    return pl.pallas_call(
        functools.partial(x_inverse_kernel, rows_y),
        out_shape=jax.ShapeDtypeStruct((dst, modes_z, per_dst, width), jnp.float32),
        scratch_shapes=[pltpu.VMEM((len(parts), modes_z, per_src, width), jnp.float32)],
        compiler_params=pltpu.CompilerParams(vmem_limit_bytes=8 << 20),
        name="x_inverse",
    )(*parts, *table)


def fold_count(rows, modes_y):
    fold = max(1, LANES // modes_y)
    return fold if rows % (OCT * fold) == 0 else 1


def fold_rows(value, fold):
    step = value.shape[-2] // fold
    return jnp.concatenate(
        [value[..., r * step : (r + 1) * step, :] for r in range(fold)], axis=-1
    )


def pack_kernel(w_ref, out_ref):
    _, parts, inputs, outputs, modes_z, local_x, modes_y = w_ref.shape
    rows = modes_z * local_x
    fold = rows // out_ref.shape[3]
    for p in range(parts):
        for c in range(inputs):
            block = w_ref[0, p, c].reshape(outputs, rows, modes_y)
            out_ref[p, c] = fold_rows(block, fold)


def pack_weights(layer, weights):
    _, parts, channels, _, modes_z, local_x, modes_y = weights.shape
    rows = modes_z * local_x
    fold = fold_count(rows, modes_y)
    per_step = 2 if channels % 2 == 0 else 1
    packed = (rows // fold, fold * modes_y)
    return pl.pallas_call(
        pack_kernel,
        grid=(channels // per_step,),
        in_specs=[
            pl.BlockSpec(
                (1, parts, per_step, channels, modes_z, local_x, modes_y),
                lambda s: (layer, 0, s, 0, 0, 0, 0),
            )
        ],
        out_specs=pl.BlockSpec((parts, per_step, channels, *packed), lambda s: (0, s, 0, 0, 0)),
        out_shape=jax.ShapeDtypeStruct((parts, channels, channels, *packed), jnp.float32),
        compiler_params=pltpu.CompilerParams(vmem_limit_bytes=30 << 20),
        cost_estimate=pl.CostEstimate(
            flops=0, bytes_accessed=5 * parts * channels * channels * rows * LANES, transcendentals=0
        ),
        name="pack_weights",
    )(weights)


def y_kernel(count_y, *refs):
    data_refs, refs = refs[:count_y], refs[count_y:]
    w_ref, f_hi, f_lo, i_hi, i_lo = refs[:5]
    out_refs, s_ref, m_ref = refs[5 : 5 + count_y], refs[-2], refs[-1]
    me = lax.axis_index("gy")
    modes_z, local_x, width = data_refs[0].shape
    groups = width // LANES
    rows = modes_z * local_x
    _, channels, _, high, wide = w_ref.shape
    fold = rows // high
    modes_y = wide // fold
    cg = channels // groups
    pair = 2 if count_y % 2 == 0 else 1

    full = None
    for first in range(0, count_y, pair):
        slots = range(first, first + pair)
        left = jnp.concatenate(
            [
                jnp.concatenate(
                    [
                        data_refs[s][:, :, g * LANES : (g + 1) * LANES].reshape(rows, LANES)
                        for g in range(groups)
                    ],
                    axis=0,
                )
                for s in slots
            ],
            axis=1,
        )
        right = [
            jnp.concatenate([t[jnp.bitwise_xor(me, s)] for s in slots], axis=0)
            for t in (f_hi, f_lo)
        ]
        term = dot3(split(left), right)
        full = term if full is None else full + term
    for g in range(groups):
        for c in range(cg):
            for q in range(2):
                start = (c * 2 + q) * modes_y
                block = full[g * rows : (g + 1) * rows, start : start + modes_y]
                s_ref[g * cg + c, q] = fold_rows(block, fold)

    for o in range(channels):
        real = imag = None
        for c in range(channels):
            wr, wi = w_ref[0, c, o], w_ref[1, c, o]
            sr, si = s_ref[c, 0], s_ref[c, 1]
            a, b = wr * sr - wi * si, wr * si + wi * sr
            real, imag = (a, b) if c == 0 else (real + a, imag + b)
        m_ref[o, 0] = real
        m_ref[o, 1] = imag

    blocks = []
    for g in range(groups):
        for r in range(fold):
            pieces = [
                m_ref[g * cg + c, q][:, r * modes_y : (r + 1) * modes_y]
                for c in range(cg)
                for q in range(2)
            ]
            blocks.append(jnp.concatenate(pieces, axis=1))
    left = split(jnp.concatenate(blocks, axis=0))
    for first in range(0, count_y, pair):
        slots = range(first, first + pair)
        right = [
            jnp.concatenate([t[jnp.bitwise_xor(me, s)] for s in slots], axis=1)
            for t in (i_hi, i_lo)
        ]
        lines = dot3(left, right)
        for at, s in enumerate(slots):
            for g in range(groups):
                piece = lines[g * rows : (g + 1) * rows, at * LANES : (at + 1) * LANES]
                out_refs[s][:, :, g * LANES : (g + 1) * LANES] = piece.reshape(
                    modes_z, local_x, LANES
                )


def y_step(parts, weights, forward, inverse):
    count_y = len(parts)
    _, channels, _, high, wide = weights.shape
    shape = jax.ShapeDtypeStruct(parts[0].shape, jnp.float32)
    return pl.pallas_call(
        functools.partial(y_kernel, count_y),
        out_shape=[shape] * count_y,
        scratch_shapes=[pltpu.VMEM((channels, 2, high, wide), jnp.float32)] * 2,
        compiler_params=pltpu.CompilerParams(vmem_limit_bytes=14 << 20),
        name="y_step",
    )(*parts, weights, *forward, *inverse)


def exchange(parts, axis):
    count = len(parts)
    moved = [parts[0]]
    for s in range(1, count):
        moved.append(lax.ppermute(parts[s], axis, [(i, i ^ s) for i in range(count)]))
    return moved


def constant_split(table):
    high = np.asarray(table, np.float32).astype(jnp.bfloat16)
    low = (np.asarray(table, np.float32) - high.astype(np.float32)).astype(jnp.bfloat16)
    return jnp.asarray(high), jnp.asarray(low)


def time_tables(rows_x, depth, total):
    cosine, sine = wave_tables(np.arange(MZ), depth)
    weight = np.where(np.arange(MZ) == 0, 1.0, 2.0)[:, None] / total
    forward = np.repeat(np.concatenate([cosine, -sine]), rows_x, axis=0).T
    inverse = np.repeat(np.concatenate([cosine * weight, -sine * weight]), rows_x, axis=0)
    return constant_split(forward), constant_split(inverse)


def x_tables(points_x, count_y):
    cosine, sine = wave_tables(mode_list(MX, points_x), points_x)
    both = np.stack([cosine.reshape(count_y, -1, points_x), sine.reshape(count_y, -1, points_x)], 1)
    forward = both.reshape(count_y, -1, points_x)
    return constant_split(forward), constant_split(np.concatenate([cosine.T, sine.T], 0))


def y_tables(points_y, rows_y):
    cosine, sine = wave_tables(mode_list(MY, points_y), points_y)
    count = points_y // rows_y
    cg = LANES // (2 * rows_y)
    cosine = cosine.reshape(MY, count, rows_y)
    sine = sine.reshape(MY, count, rows_y)
    fwd = np.stack([np.stack([cosine, -sine]), np.stack([sine, cosine])])
    inv = np.stack([np.stack([cosine, sine]), np.stack([-sine, cosine])])
    eye = np.eye(cg)
    fwd = np.einsum("ab,rqmgy->garybqm", eye, fwd).reshape(count, LANES, cg * 2 * MY)
    inv = np.einsum("ab,qrmgy->gaqmbry", eye, inv).reshape(count, cg * 2 * MY, LANES)
    return constant_split(fwd), constant_split(inv)


def shards(field, spectral_weight, point_weight, bias):
    channels, rows_x, rows_y, depth = field.shape
    layers = spectral_weight.shape[0]
    count_x = lax.axis_size("gx")
    count_y = lax.axis_size("gy")
    points_x = rows_x * count_x
    points_y = rows_y * count_y
    local_z = MZ // count_x
    fwd_z, inv_z = time_tables(rows_x, depth, float(points_x * points_y * depth))
    fwd_x, inv_x = x_tables(points_x, count_y)
    fwd_y, inv_y = y_tables(points_y, rows_y)
    tables = {"fwd": fwd_z, "inv": inv_z}
    last = {"fwd": None, "inv": inv_z}
    packed = [pack_weights(layer, spectral_weight) for layer in range(layers)]

    current = field
    (spectrum,) = time_step(0, current, None, tables, point_weight, bias)
    for layer in range(layers):
        data = spectrum.reshape(count_x, local_z, rows_x, -1)
        data = lax.all_to_all(data, "gx", 0, 0)
        parts = exchange(x_forward(rows_y, data, fwd_x), "gy")
        parts = exchange(y_step(parts, packed[layer], fwd_y, inv_y), "gy")
        data = x_inverse(rows_y, parts, inv_x, count_x)
        data = lax.all_to_all(data, "gx", 0, 0)
        planes = data.reshape(MZ, rows_x, -1)
        if layer + 1 < layers:
            current, spectrum = time_step(layer, current, planes, tables, point_weight, bias)
        else:
            (current,) = time_step(layer, current, planes, last, point_weight, bias)
    return current


def solution(mesh):
    return jax.shard_map(
        shards,
        mesh=mesh,
        in_specs=(P(None, "gx", "gy", None), P(None, None, None, None, "gx", "gy", None), P(), P()),
        out_specs=P(None, "gx", "gy", None),
        check_vma=False,
    )
```

```python
import functools

import jax
import jax.numpy as jnp
import numpy as np
from jax import lax
from jax.experimental import pallas as pl
from jax.experimental.pallas import tpu as pltpu
from jax.sharding import PartitionSpec as P

MZ = 16
MX = 64
MY = 32
LANES = 128
OCT = 8
AT_ONCE = 4


def mode_list(count, points):
    half = count // 2
    lower = np.arange(half)
    return np.concatenate([lower, points - half + lower])


def wave_tables(modes, points):
    phase = 2.0 * np.pi / points * ((modes[:, None] * np.arange(points)[None, :]) % points)
    return np.cos(phase), np.sin(phase)


def split(value):
    high = value.astype(jnp.bfloat16)
    low = (value - high.astype(jnp.float32)).astype(jnp.bfloat16)
    return high, low


def dot3(left, right):
    def one(a, b):
        return jnp.dot(a, b, preferred_element_type=jnp.float32)

    return one(left[0], right[0]) + one(left[1], right[0]) + one(left[0], right[1])


def time_kernel(layer, has_inverse, has_forward, *refs):
    refs = list(refs)
    u_ref = refs.pop(0)
    if has_inverse:
        planes_ref, inv_ref, point_ref, bias_ref = (refs.pop(0) for _ in range(4))
    if has_forward:
        fwd_ref = refs.pop(0)
    if has_inverse:
        out_ref = refs.pop(0)
    if has_forward:
        spec_ref = refs.pop(0)
    if has_inverse:
        p_hi, p_lo, mix_hi, mix_lo, wide_bias = (refs.pop(0) for _ in range(5))
    if has_forward:
        acc = refs.pop(0)
    step = pl.program_id(0)
    channels, at_once, rows_y, depth = u_ref.shape
    rows_x = pl.num_programs(0) * at_once
    cg = LANES // (2 * rows_y)
    groups = channels // cg

    if has_inverse:

        @pl.when(step == 0)
        def _():
            modes, local, width = planes_ref.shape
            n = modes * local
            flat = planes_ref[...].reshape(n, width)
            for g in range(groups):
                turned = flat[:, g * LANES : (g + 1) * LANES].T
                high, low = split(turned)
                for c in range(cg):
                    for q in range(2):
                        src = slice((c * 2 + q) * rows_y, (c * 2 + q + 1) * rows_y)
                        dst = slice((g * cg + c) * rows_y, (g * cg + c + 1) * rows_y)
                        p_hi[dst, q * n : (q + 1) * n] = high[src]
                        p_lo[dst, q * n : (q + 1) * n] = low[src]
            side = channels * OCT
            pick = lax.broadcasted_iota(jnp.int32, (side, channels), 0) // OCT
            pick = (pick == lax.broadcasted_iota(jnp.int32, (side, channels), 1)).astype(
                jnp.bfloat16
            )
            place = lax.broadcasted_iota(jnp.int32, (channels, side), 1) // OCT
            place = (place == lax.broadcasted_iota(jnp.int32, (channels, side), 0)).astype(
                jnp.bfloat16
            )
            same = lax.broadcasted_iota(jnp.int32, (side, side), 0) % OCT
            same = same == lax.broadcasted_iota(jnp.int32, (side, side), 1) % OCT
            contract = (((1,), (1,)), ((), ()))
            for part, target in zip(split(point_ref[layer]), (mix_hi, mix_lo)):
                rows = lax.dot_general(pick, part, contract, preferred_element_type=jnp.float32)
                full = jnp.dot(
                    rows.astype(jnp.bfloat16), place, preferred_element_type=jnp.float32
                )
                target[...] = jnp.where(same, full, 0.0).astype(jnp.bfloat16)
            lines = jnp.broadcast_to(bias_ref[layer : layer + 1, :], (LANES, channels))
            first = lines.astype(jnp.bfloat16)
            rest = lines - first.astype(jnp.float32)
            second, third = split(rest)
            wide_bias[...] = sum(
                lax.dot_general(pick, part, contract, preferred_element_type=jnp.float32)
                for part in (third, second, first)
            )

        n2 = p_hi.shape[1]
        lane = lax.broadcasted_iota(jnp.int32, (OCT, n2), 1) % rows_x
        left = []
        for part in (p_hi, p_lo):
            pieces = []
            for i in range(at_once):
                keep = jnp.where(lane == step * at_once + i, 1.0, 0.0).astype(jnp.bfloat16)[0:1]
                pieces.append(part[...] * keep)
            left.append(jnp.concatenate(pieces, axis=0))
        wave = dot3(left, (inv_ref[0], inv_ref[1]))
        wave = wave.reshape(at_once, channels, rows_y, depth)
        mixer = (mix_hi[...], mix_lo[...])
        shift = jnp.concatenate([wide_bias[...]] * (depth // LANES), axis=1)
        for i in range(at_once):
            for part in range(rows_y // OCT):
                rows = slice(part * OCT, (part + 1) * OCT)
                x = u_ref[:, i, rows, :].reshape(channels * OCT, depth)
                local = dot3(mixer, split(x))
                v = wave[i, :, rows, :].reshape(channels * OCT, depth) + local + shift
                v = v * (lax.erf(v * np.float32(np.sqrt(0.5))) + 1.0) * 0.5
                out_ref[:, i, rows, :] = v.reshape(channels, OCT, depth)

    if has_forward:
        source = out_ref if has_inverse else u_ref
        count = channels * rows_y
        values = [source[:, i, :, :].reshape(count, depth) for i in range(at_once)]
        terms = dot3(split(jnp.concatenate(values, axis=0)), (fwd_ref[0], fwd_ref[1]))
        lane = lax.broadcasted_iota(jnp.int32, (count, terms.shape[1]), 1) % rows_x
        term = terms[:count]
        for i in range(1, at_once):
            term = jnp.where(lane == step * at_once + i, terms[i * count : (i + 1) * count], term)

        @pl.when(step == 0)
        def _():
            acc[...] = term

        @pl.when(step > 0)
        def _():
            acc[...] = jnp.where(lane >= step * at_once, term, acc[...])

        @pl.when(step == pl.num_programs(0) - 1)
        def _():
            modes, local, width = spec_ref.shape
            n = modes * local
            for g in range(groups):
                pieces = []
                for c in range(cg):
                    for q in range(2):
                        rows = slice((g * cg + c) * rows_y, (g * cg + c + 1) * rows_y)
                        pieces.append(acc[rows, q * n : (q + 1) * n])
                turned = jnp.concatenate(pieces, axis=0).T
                spec_ref[:, :, g * LANES : (g + 1) * LANES] = turned.reshape(modes, local, LANES)


def time_step(layer, u, planes, tables, point_weight, bias):
    channels, rows_x, rows_y, depth = u.shape
    has_inverse = planes is not None
    has_forward = tables["fwd"] is not None
    width = channels * 2 * rows_y
    n = MZ * rows_x
    side = channels * OCT
    at_once = AT_ONCE if rows_x % AT_ONCE == 0 else 1
    block = pl.BlockSpec((channels, at_once, rows_y, depth), lambda s: (0, s, 0, 0))

    def whole(shape):
        return pl.BlockSpec(shape, lambda s: (0,) * len(shape))

    args, specs = [u], [block]
    if has_inverse:
        rest = [planes, tables["inv"], point_weight, bias]
        args += rest
        specs += [whole(a.shape) for a in rest]
    if has_forward:
        args += [tables["fwd"]]
        specs += [whole(tables["fwd"].shape)]
    outs, out_specs, scratch = [], [], []
    if has_inverse:
        outs.append(jax.ShapeDtypeStruct(u.shape, jnp.float32))
        out_specs.append(block)
        scratch += [pltpu.VMEM((channels * rows_y, 2 * n), jnp.bfloat16)] * 2
        scratch += [pltpu.VMEM((side, side), jnp.bfloat16)] * 2
        scratch += [pltpu.VMEM((side, LANES), jnp.float32)]
    if has_forward:
        outs.append(jax.ShapeDtypeStruct((MZ, rows_x, width), jnp.float32))
        out_specs.append(whole((MZ, rows_x, width)))
        scratch += [pltpu.VMEM((channels * rows_y, 2 * n), jnp.float32)]
    return pl.pallas_call(
        functools.partial(time_kernel, layer, has_inverse, has_forward),
        grid=(rows_x // at_once,),
        in_specs=specs,
        out_specs=out_specs,
        out_shape=outs,
        scratch_shapes=scratch,
        compiler_params=pltpu.CompilerParams(vmem_limit_bytes=14 << 20),
        name="time_step",
    )(*args)


def turn(sign, rows_y, cosine, sine):
    lane = lax.broadcasted_iota(jnp.int32, cosine.shape, 1)
    ahead = pltpu.roll(sine, LANES - rows_y, axis=1)
    behind = pltpu.roll(sine, rows_y, axis=1)
    swapped = jnp.where((lane // rows_y) % 2 == 0, ahead, -behind)
    return cosine + swapped if sign > 0 else cosine - swapped


def x_forward_kernel(rows_y, data_ref, t_ref, *out_refs):
    me = lax.axis_index("gy")
    src, modes_z, per_src, width = data_ref.shape
    _, per_dst, _ = out_refs[0].shape
    table = [
        jnp.concatenate([t_ref[p, jnp.bitwise_xor(me, s)] for s in range(len(out_refs))], axis=0)
        for p in range(2)
    ]
    for k in range(modes_z):
        both = dot3(table, split(data_ref[:, k].reshape(src * per_src, width)))
        for s, out_ref in enumerate(out_refs):
            top = 2 * s * per_dst
            for g in range(width // LANES):
                cols = slice(g * LANES, (g + 1) * LANES)
                cosine = both[top : top + per_dst, cols]
                sine = both[top + per_dst : top + 2 * per_dst, cols]
                out_ref[k, :, cols] = turn(1, rows_y, cosine, sine)


def x_forward(rows_y, data, table):
    src, modes_z, per_src, width = data.shape
    _, count_y, twice, _ = table.shape
    return pl.pallas_call(
        functools.partial(x_forward_kernel, rows_y),
        out_shape=[jax.ShapeDtypeStruct((modes_z, twice // 2, width), jnp.float32)] * count_y,
        compiler_params=pltpu.CompilerParams(vmem_limit_bytes=8 << 20),
        name="x_forward",
    )(data, table)


def x_inverse_kernel(rows_y, *refs):
    *data_refs, t_ref, out_ref, work = refs
    me = lax.axis_index("gy")
    for s, data_ref in enumerate(data_refs):
        work[jnp.bitwise_xor(me, s)] = data_ref[...]
    src, modes_z, per_src, width = work.shape
    dst, _, per_dst, _ = out_ref.shape
    n = dst * per_dst
    table = (t_ref[0], t_ref[1])
    for k in range(modes_z):
        both = dot3(table, split(work[:, k].reshape(src * per_src, width)))
        for g in range(width // LANES):
            cols = slice(g * LANES, (g + 1) * LANES)
            value = turn(-1, rows_y, both[:n, cols], both[n:, cols])
            out_ref[:, k, :, cols] = value.reshape(dst, per_dst, LANES)


def x_inverse(rows_y, parts, table, dst):
    modes_z, per_src, width = parts[0].shape
    per_dst = table.shape[1] // 2 // dst
    return pl.pallas_call(
        functools.partial(x_inverse_kernel, rows_y),
        out_shape=jax.ShapeDtypeStruct((dst, modes_z, per_dst, width), jnp.float32),
        scratch_shapes=[pltpu.VMEM((len(parts), modes_z, per_src, width), jnp.float32)],
        compiler_params=pltpu.CompilerParams(vmem_limit_bytes=8 << 20),
        name="x_inverse",
    )(*parts, table)


def fold_count(rows, modes_y):
    fold = max(1, LANES // modes_y)
    return fold if rows % (OCT * fold) == 0 else 1


def fold_rows(value, fold):
    step = value.shape[-2] // fold
    return jnp.concatenate(
        [value[..., r * step : (r + 1) * step, :] for r in range(fold)], axis=-1
    )


def pack_kernel(layer, start, w_ref, out_ref, held, sems):
    parts, inputs, outputs, high, _ = out_ref.shape
    modes_z, local_x, modes_y = held.shape[-3:]
    rows = modes_z * local_x

    def fetch(c, p):
        return pltpu.make_async_copy(
            w_ref.at[layer, p, start + c], held.at[c, p], sems.at[c, p]
        )

    @pl.loop(0, inputs)
    def _(c):
        for p in range(parts):
            fetch(c, p).start()

    @pl.loop(0, inputs)
    def _(c):
        for p in range(parts):
            fetch(c, p).wait()
            block = held[c, p].reshape(outputs, rows, modes_y)
            out_ref[p, c] = fold_rows(block, rows // high)


def pack_weights(layer, start, inputs, weights):
    _, parts, channels, _, modes_z, local_x, modes_y = weights.shape
    rows = modes_z * local_x
    fold = fold_count(rows, modes_y)
    packed = (rows // fold, fold * modes_y)
    return pl.pallas_call(
        functools.partial(pack_kernel, layer, start),
        in_specs=[pl.BlockSpec(memory_space=pl.ANY)],
        out_shape=jax.ShapeDtypeStruct((parts, inputs, channels, *packed), jnp.float32),
        scratch_shapes=[
            pltpu.VMEM((inputs, parts, channels, modes_z, local_x, modes_y), jnp.float32),
            pltpu.SemaphoreType.DMA((inputs, parts)),
        ],
        compiler_params=pltpu.CompilerParams(vmem_limit_bytes=28 << 20),
        cost_estimate=pl.CostEstimate(
            flops=0, bytes_accessed=5 * parts * inputs * channels * rows * LANES, transcendentals=0
        ),
        name="pack_weights",
    )(weights)


def y_kernel(count_y, *refs):
    data_refs, refs = refs[:count_y], refs[count_y:]
    *w_refs, f_ref, i_ref = refs[: -count_y - 2]
    out_refs, s_ref, m_ref = refs[-count_y - 2 : -2], refs[-2], refs[-1]
    inputs = [(w_ref, c) for w_ref in w_refs for c in range(w_ref.shape[1])]
    me = lax.axis_index("gy")
    modes_z, local_x, width = data_refs[0].shape
    groups = width // LANES
    rows = modes_z * local_x
    _, _, channels, high, wide = w_refs[0].shape
    fold = rows // high
    modes_y = wide // fold
    cg = channels // groups
    pair = 2 if count_y % 2 == 0 else 1

    full = None
    for first in range(0, count_y, pair):
        slots = range(first, first + pair)
        left = jnp.concatenate(
            [
                jnp.concatenate(
                    [
                        data_refs[s][:, :, g * LANES : (g + 1) * LANES].reshape(rows, LANES)
                        for g in range(groups)
                    ],
                    axis=0,
                )
                for s in slots
            ],
            axis=1,
        )
        right = [
            jnp.concatenate([f_ref[p, jnp.bitwise_xor(me, s)] for s in slots], axis=0)
            for p in range(2)
        ]
        term = dot3(split(left), right)
        full = term if full is None else full + term
    for g in range(groups):
        for c in range(cg):
            for q in range(2):
                start = (c * 2 + q) * modes_y
                block = full[g * rows : (g + 1) * rows, start : start + modes_y]
                s_ref[g * cg + c, q] = fold_rows(block, fold)

    for o in range(channels):
        real = imag = None
        for c, (w_ref, at) in enumerate(inputs):
            wr, wi = w_ref[0, at, o], w_ref[1, at, o]
            sr, si = s_ref[c, 0], s_ref[c, 1]
            a, b = wr * sr - wi * si, wr * si + wi * sr
            real, imag = (a, b) if c == 0 else (real + a, imag + b)
        m_ref[o, 0] = real
        m_ref[o, 1] = imag

    blocks = []
    for g in range(groups):
        for r in range(fold):
            pieces = [
                m_ref[g * cg + c, q][:, r * modes_y : (r + 1) * modes_y]
                for c in range(cg)
                for q in range(2)
            ]
            blocks.append(jnp.concatenate(pieces, axis=1))
    left = split(jnp.concatenate(blocks, axis=0))
    for first in range(0, count_y, pair):
        slots = range(first, first + pair)
        right = [
            jnp.concatenate([i_ref[p, jnp.bitwise_xor(me, s)] for s in slots], axis=1)
            for p in range(2)
        ]
        lines = dot3(left, right)
        for at, s in enumerate(slots):
            for g in range(groups):
                piece = lines[g * rows : (g + 1) * rows, at * LANES : (at + 1) * LANES]
                out_refs[s][:, :, g * LANES : (g + 1) * LANES] = piece.reshape(
                    modes_z, local_x, LANES
                )


def y_step(parts, weights, forward, inverse):
    count_y = len(parts)
    _, _, channels, high, wide = weights[0].shape
    shape = jax.ShapeDtypeStruct(parts[0].shape, jnp.float32)
    return pl.pallas_call(
        functools.partial(y_kernel, count_y),
        out_shape=[shape] * count_y,
        scratch_shapes=[pltpu.VMEM((channels, 2, high, wide), jnp.float32)] * 2,
        compiler_params=pltpu.CompilerParams(vmem_limit_bytes=14 << 20),
        name="y_step",
    )(*parts, *weights, forward, inverse)


def exchange(parts, axis):
    count = len(parts)
    moved = [parts[0]]
    for s in sorted(range(1, count), key=lambda s: (s < 2, s)):
        moved.append(lax.ppermute(parts[s], axis, [(i, i ^ s) for i in range(count)]))
    return [moved[0], moved[-1], *moved[1:-1]]


def constant_split(table):
    high = np.asarray(table, np.float32).astype(jnp.bfloat16)
    low = (np.asarray(table, np.float32) - high.astype(np.float32)).astype(jnp.bfloat16)
    return jnp.asarray(np.stack([high, low]))


def time_tables(rows_x, depth, total):
    cosine, sine = wave_tables(np.arange(MZ), depth)
    weight = np.where(np.arange(MZ) == 0, 1.0, 2.0)[:, None] / total
    forward = np.repeat(np.concatenate([cosine, -sine]), rows_x, axis=0).T
    inverse = np.repeat(np.concatenate([cosine * weight, -sine * weight]), rows_x, axis=0)
    return constant_split(forward), constant_split(inverse)


def x_tables(points_x, count_y):
    cosine, sine = wave_tables(mode_list(MX, points_x), points_x)
    both = np.stack([cosine.reshape(count_y, -1, points_x), sine.reshape(count_y, -1, points_x)], 1)
    forward = both.reshape(count_y, -1, points_x)
    return constant_split(forward), constant_split(np.concatenate([cosine.T, sine.T], 0))


def y_tables(points_y, rows_y):
    cosine, sine = wave_tables(mode_list(MY, points_y), points_y)
    count = points_y // rows_y
    cg = LANES // (2 * rows_y)
    cosine = cosine.reshape(MY, count, rows_y)
    sine = sine.reshape(MY, count, rows_y)
    fwd = np.stack([np.stack([cosine, -sine]), np.stack([sine, cosine])])
    inv = np.stack([np.stack([cosine, sine]), np.stack([-sine, cosine])])
    eye = np.eye(cg)
    fwd = np.einsum("ab,rqmgy->garybqm", eye, fwd).reshape(count, LANES, cg * 2 * MY)
    inv = np.einsum("ab,qrmgy->gaqmbry", eye, inv).reshape(count, cg * 2 * MY, LANES)
    return constant_split(fwd), constant_split(inv)


def shards(field, spectral_weight, point_weight, bias):
    channels, rows_x, rows_y, depth = field.shape
    layers = spectral_weight.shape[0]
    count_x = lax.axis_size("gx")
    count_y = lax.axis_size("gy")
    points_x = rows_x * count_x
    points_y = rows_y * count_y
    local_z = MZ // count_x
    fwd_z, inv_z = time_tables(rows_x, depth, float(points_x * points_y * depth))
    fwd_x, inv_x = x_tables(points_x, count_y)
    fwd_y, inv_y = y_tables(points_y, rows_y)
    tables = {"fwd": fwd_z, "inv": inv_z}
    last = {"fwd": None, "inv": inv_z}
    half = channels // 2
    shares = ((0, half), (half, channels - half))

    def pack(layer, share):
        return pack_weights(layer, *shares[share], spectral_weight)

    current = field
    first = pltpu.with_memory_space_constraint(field, pltpu.HBM)
    (spectrum,) = time_step(0, first, None, tables, point_weight, bias)
    weights = []
    for layer in range(layers):
        data = spectrum.reshape(count_x, local_z, rows_x, -1)
        data = lax.all_to_all(data, "gx", 0, 0)
        parts = exchange(x_forward(rows_y, data, fwd_x), "gy")
        weights.append(pack(layer, 1) if weights else pack_weights(layer, 0, channels, spectral_weight))
        parts = exchange(y_step(parts, weights, fwd_y, inv_y), "gy")
        if layer + 1 < layers:
            parts, early = lax.optimization_barrier((parts, pack(layer + 1, 0)))
            weights = [early]
        data = x_inverse(rows_y, parts, inv_x, count_x)
        data = lax.all_to_all(data, "gx", 0, 0)
        planes = data.reshape(MZ, rows_x, -1)
        if layer + 1 < layers:
            current, spectrum = time_step(layer, current, planes, tables, point_weight, bias)
        else:
            (current,) = time_step(layer, current, planes, last, point_weight, bias)
    return current


def solution(mesh):
    return jax.shard_map(
        shards,
        mesh=mesh,
        in_specs=(P(None, "gx", "gy", None), P(None, None, None, None, "gx", "gy", None), P(), P()),
        out_specs=P(None, "gx", "gy", None),
        check_vma=False,
    )
```

```python
import functools

import jax
import jax.numpy as jnp
import numpy as np
from jax import lax
from jax.experimental import pallas as pl
from jax.experimental.pallas import tpu as pltpu
from jax.sharding import PartitionSpec as P

MZ = 16
MX = 64
MY = 32
LANES = 128
OCT = 8


def mode_list(count, points):
    half = count // 2
    lower = np.arange(half)
    return np.concatenate([lower, points - half + lower])


def wave_tables(modes, points):
    phase = 2.0 * np.pi / points * ((modes[:, None] * np.arange(points)[None, :]) % points)
    return np.cos(phase), np.sin(phase)


def split(value):
    high = value.astype(jnp.bfloat16)
    low = (value - high.astype(jnp.float32)).astype(jnp.bfloat16)
    return high, low


def stack_rows(value):
    high, low = split(value)
    return jnp.concatenate([high, high, low], axis=0)


def dot3(left, right):
    def one(a, b):
        return jnp.dot(a, b, preferred_element_type=jnp.float32)

    return one(left[0], right[0]) + one(left[1], right[0]) + one(left[0], right[1])


def forward_rows(values, fwd_ref, rows_x):
    half = len(values)
    count = values[0].shape[0]
    high, low = split(jnp.concatenate(values, axis=0))
    one = jnp.dot(high, fwd_ref[0], preferred_element_type=jnp.float32)
    two = jnp.dot(low, fwd_ref[1], preferred_element_type=jnp.float32)
    lane = lax.broadcasted_iota(jnp.int32, (count, one.shape[1]), 1)
    picked = []
    for product in (one, two):
        total = product[:count]
        for i in range(1, half):
            here = product[i * count : (i + 1) * count]
            total = jnp.where(lane % half == i, here, total)
        picked.append(total)
    one, two = picked
    width = one.shape[1]
    other = jnp.where(
        lane % rows_x < half, pltpu.roll(one, width - half, axis=1), pltpu.roll(one, half, axis=1)
    )
    return one + other + two, lane % rows_x // half


def write_spectrum(acc, spec_ref, channels, rows_y):
    modes, local, width = spec_ref.shape
    n = modes * local
    cg = LANES // (2 * rows_y)
    for g in range(channels // cg):
        pieces = []
        for c in range(cg):
            for q in range(2):
                rows = slice((g * cg + c) * rows_y, (g * cg + c + 1) * rows_y)
                pieces.append(acc[rows, q * n : (q + 1) * n])
        turned = jnp.concatenate(pieces, axis=0).T
        spec_ref[:, :, g * LANES : (g + 1) * LANES] = turned.reshape(modes, local, LANES)


def first_kernel(u_ref, fwd_any, spec_ref, held, fwd_ref, acc, sems, table_sem):
    rows_x, channels, rows_y, depth = held.shape
    count = channels * rows_y
    table = pltpu.make_async_copy(fwd_any, fwd_ref, table_sem.at[0])

    def fetch(x):
        return pltpu.make_async_copy(u_ref.at[:, x], held.at[x], sems.at[x])

    table.start()
    for x in range(rows_x):
        fetch(x).start()
    table.wait()
    half = rows_x // 2
    for part in range(2):
        values = []
        for x in range(part * half, (part + 1) * half):
            fetch(x).wait()
            values.append(held[x].reshape(count, depth))
        term, owner = forward_rows(values, fwd_ref, rows_x)
        acc[...] = term if part == 0 else jnp.where(owner == part, term, acc[...])
    write_spectrum(acc, spec_ref, channels, rows_y)


def first_step(u, table):
    channels, rows_x, rows_y, depth = u.shape
    n = MZ * rows_x
    return pl.pallas_call(
        first_kernel,
        in_specs=[pl.BlockSpec(memory_space=pl.ANY)] * 2,
        out_shape=jax.ShapeDtypeStruct((MZ, rows_x, channels * 2 * rows_y), jnp.float32),
        scratch_shapes=[
            pltpu.VMEM((rows_x, channels, rows_y, depth), jnp.float32),
            pltpu.VMEM(table.shape, table.dtype),
            pltpu.VMEM((channels * rows_y, 2 * n), jnp.float32),
            pltpu.SemaphoreType.DMA((rows_x,)),
            pltpu.SemaphoreType.DMA((1,)),
        ],
        compiler_params=pltpu.CompilerParams(vmem_limit_bytes=14 << 20),
        name="first_step",
    )(u, table)


def point_tables(layer, point_ref, bias_ref, mix_ref, wide_bias):
    channels = point_ref.shape[1]
    side = channels * OCT
    pick = lax.broadcasted_iota(jnp.int32, (side, channels), 0) // OCT
    pick = (pick == lax.broadcasted_iota(jnp.int32, (side, channels), 1)).astype(jnp.bfloat16)
    column = lax.broadcasted_iota(jnp.int32, (channels, 3 * side), 1) % side // OCT
    place = column == lax.broadcasted_iota(jnp.int32, (channels, 3 * side), 0)
    place = place.astype(jnp.bfloat16)
    column = lax.broadcasted_iota(jnp.int32, (side, 3 * side), 1)
    same = lax.broadcasted_iota(jnp.int32, (side, 3 * side), 0) % OCT == column % OCT
    contract = (((1,), (1,)), ((), ()))
    full = []
    for part in split(point_ref[layer]):
        rows = lax.dot_general(pick, part, contract, preferred_element_type=jnp.float32)
        full.append(
            jnp.dot(rows.astype(jnp.bfloat16), place, preferred_element_type=jnp.float32)
        )
    value = jnp.where((column >= side) & (column < 2 * side), full[1], full[0])
    mix_ref[...] = jnp.where(same, value, 0.0).astype(jnp.bfloat16)
    lines = jnp.broadcast_to(bias_ref[layer : layer + 1, :], (LANES, channels))
    first = lines.astype(jnp.bfloat16)
    second, third = split(lines - first.astype(jnp.float32))
    wide_bias[...] = sum(
        lax.dot_general(pick, part, contract, preferred_element_type=jnp.float32)
        for part in (third, second, first)
    )


def turn_planes(planes_ref, p_ref, channels, rows_y):
    cg = LANES // (2 * rows_y)
    groups = channels // cg
    rows_x = planes_ref.shape[0] // (MZ * groups)
    per = LANES // (4 * MZ)
    for pair in range(rows_x // per):
        for g in range(groups):
            pieces = []
            for x in range(pair * per, (pair + 1) * per):
                value = planes_ref[pl.ds(g * rows_x + x, MZ, stride=groups * rows_x), :]
                high = value.astype(jnp.bfloat16).astype(jnp.float32)
                pieces += [high, value - high, high, jnp.zeros_like(high)]
            turned = jnp.concatenate(pieces, axis=0).T.astype(jnp.bfloat16)
            for c in range(cg):
                for q in range(2):
                    src = slice((c * 2 + q) * rows_y, (c * 2 + q + 1) * rows_y)
                    dst = slice((g * cg + c) * rows_y, (g * cg + c + 1) * rows_y)
                    p_ref[pair, dst, q * LANES : (q + 1) * LANES] = turned[src]


def time_kernel(layer, has_forward, *refs):
    u_ref, planes_ref, inv_ref, point_ref, bias_ref, *refs = refs
    if has_forward:
        fwd_ref, out_ref, spec_ref, p_ref, mix_ref, wide_bias, acc = refs
    else:
        out_ref, p_ref, mix_ref, wide_bias = refs
    step = pl.program_id(0)
    channels, at_once, rows_y, depth = u_ref.shape
    rows_x = pl.num_programs(0) * at_once
    count = channels * rows_y
    per = inv_ref.shape[0]
    pairs = at_once // per

    @pl.when(step == 0)
    def _():
        turn_planes(planes_ref, p_ref, channels, rows_y)
        point_tables(layer, point_ref, bias_ref, mix_ref, wide_bias)

    left = jnp.concatenate([p_ref[step * pairs + i] for i in range(pairs)], axis=0)
    waves = [jnp.dot(left, inv_ref[h], preferred_element_type=jnp.float32) for h in range(per)]
    mixer = mix_ref[...]
    shift = jnp.concatenate([wide_bias[...]] * (depth // LANES), axis=1)
    for i in range(at_once):
        wave = waves[i % per][(i // per) * count : (i // per + 1) * count]
        wave = wave.reshape(channels, rows_y, depth)
        for part in range(rows_y // OCT):
            rows = slice(part * OCT, (part + 1) * OCT)
            x = u_ref[:, i, rows, :].reshape(channels * OCT, depth)
            local = jnp.dot(mixer, stack_rows(x), preferred_element_type=jnp.float32)
            v = wave[:, rows, :].reshape(channels * OCT, depth) + local + shift
            v = v * (lax.erf(v * np.float32(np.sqrt(0.5))) + 1.0) * 0.5
            out_ref[:, i, rows, :] = v.reshape(channels, OCT, depth)

    if has_forward:
        values = [out_ref[:, i, :, :].reshape(count, depth) for i in range(at_once)]
        term, owner = forward_rows(values, fwd_ref, rows_x)

        @pl.when(step == 0)
        def _():
            acc[...] = term

        @pl.when(step == 1)
        def _():
            acc[...] = jnp.where(owner == 1, term, acc[...])

        @pl.when(step == pl.num_programs(0) - 1)
        def _():
            write_spectrum(acc, spec_ref, channels, rows_y)


def time_step(layer, u, planes, inverse, forward, point_weight, bias):
    channels, rows_x, rows_y, depth = u.shape
    has_forward = forward is not None
    width = channels * 2 * rows_y
    n = MZ * rows_x
    side = channels * OCT
    per = inverse.shape[0]
    at_once = rows_x // 2
    block = pl.BlockSpec((channels, at_once, rows_y, depth), lambda s: (0, s, 0, 0))

    def whole(shape):
        return pl.BlockSpec(shape, lambda s: (0,) * len(shape))

    rest = [planes, inverse, point_weight, bias] + ([forward] if has_forward else [])
    outs, out_specs = [jax.ShapeDtypeStruct(u.shape, jnp.float32)], [block]
    scratch = [
        pltpu.VMEM((rows_x // per, channels * rows_y, 2 * LANES), jnp.bfloat16),
        pltpu.VMEM((side, 3 * side), jnp.bfloat16),
        pltpu.VMEM((side, LANES), jnp.float32),
    ]
    if has_forward:
        outs.append(jax.ShapeDtypeStruct((MZ, rows_x, width), jnp.float32))
        out_specs.append(whole((MZ, rows_x, width)))
        scratch += [pltpu.VMEM((channels * rows_y, 2 * n), jnp.float32)]
    return pl.pallas_call(
        functools.partial(time_kernel, layer, has_forward),
        grid=(rows_x // at_once,),
        in_specs=[block] + [whole(a.shape) for a in rest],
        out_specs=out_specs,
        out_shape=outs,
        scratch_shapes=scratch,
        compiler_params=pltpu.CompilerParams(vmem_limit_bytes=14 << 20),
        name="time_step",
    )(u, *rest)


def turn(sign, rows_y, cosine, sine):
    lane = lax.broadcasted_iota(jnp.int32, cosine.shape, 1)
    ahead = pltpu.roll(sine, LANES - rows_y, axis=1)
    behind = pltpu.roll(sine, rows_y, axis=1)
    swapped = jnp.where((lane // rows_y) % 2 == 0, ahead, -behind)
    return cosine + swapped if sign > 0 else cosine - swapped


def x_forward_kernel(rows_y, data_ref, t_ref, *out_refs):
    me = lax.axis_index("gy")
    src, modes_z, per_src, width = data_ref.shape
    _, per_dst, _ = out_refs[0].shape
    table = jnp.concatenate([t_ref[jnp.bitwise_xor(me, s)] for s in range(len(out_refs))], axis=0)
    for k in range(modes_z):
        data = stack_rows(data_ref[:, k].reshape(src * per_src, width))
        both = jnp.dot(table, data, preferred_element_type=jnp.float32)
        for s, out_ref in enumerate(out_refs):
            top = 2 * s * per_dst
            for g in range(width // LANES):
                cols = slice(g * LANES, (g + 1) * LANES)
                cosine = both[top : top + per_dst, cols]
                sine = both[top + per_dst : top + 2 * per_dst, cols]
                out_ref[k, :, cols] = turn(1, rows_y, cosine, sine)


def x_forward(rows_y, data, table):
    src, modes_z, per_src, width = data.shape
    count_y, twice, _ = table.shape
    return pl.pallas_call(
        functools.partial(x_forward_kernel, rows_y),
        out_shape=[jax.ShapeDtypeStruct((modes_z, twice // 2, width), jnp.float32)] * count_y,
        compiler_params=pltpu.CompilerParams(vmem_limit_bytes=8 << 20),
        name="x_forward",
    )(data, table)


def x_inverse_kernel(rows_y, *refs):
    *data_refs, t_ref, out_ref, work = refs
    me = lax.axis_index("gy")
    for s, data_ref in enumerate(data_refs):
        work[jnp.bitwise_xor(me, s)] = data_ref[...]
    src, modes_z, per_src, width = work.shape
    dst, _, _, per_dst, _ = out_ref.shape
    n = dst * per_dst
    table = t_ref[...]
    for k in range(modes_z):
        data = stack_rows(work[:, k].reshape(src * per_src, width))
        both = jnp.dot(table, data, preferred_element_type=jnp.float32)
        for g in range(width // LANES):
            cols = slice(g * LANES, (g + 1) * LANES)
            value = turn(-1, rows_y, both[:n, cols], both[n:, cols])
            out_ref[:, k, g] = value.reshape(dst, per_dst, LANES)


def x_inverse(rows_y, parts, table, dst):
    modes_z, per_src, width = parts[0].shape
    per_dst = table.shape[0] // 2 // dst
    return pl.pallas_call(
        functools.partial(x_inverse_kernel, rows_y),
        out_shape=jax.ShapeDtypeStruct(
            (dst, modes_z, width // LANES, per_dst, LANES), jnp.float32
        ),
        scratch_shapes=[pltpu.VMEM((len(parts), modes_z, per_src, width), jnp.float32)],
        compiler_params=pltpu.CompilerParams(vmem_limit_bytes=8 << 20),
        name="x_inverse",
    )(*parts, table)


def fold_count(rows, modes_y):
    fold = max(1, LANES // modes_y)
    return fold if rows % (OCT * fold) == 0 else 1


def fold_rows(value, fold):
    step = value.shape[-2] // fold
    return jnp.concatenate(
        [value[..., r * step : (r + 1) * step, :] for r in range(fold)], axis=-1
    )


def pack_kernel(layer, start, w_ref, out_ref, held, sems):
    parts, inputs, outputs, high, _ = out_ref.shape
    modes_z, local_x, modes_y = held.shape[-3:]
    rows = modes_z * local_x

    def fetch(c, p):
        return pltpu.make_async_copy(
            w_ref.at[layer, p, start + c], held.at[c, p], sems.at[c, p]
        )

    @pl.loop(0, inputs)
    def _(c):
        for p in range(parts):
            fetch(c, p).start()

    @pl.loop(0, inputs)
    def _(c):
        for p in range(parts):
            fetch(c, p).wait()
            block = held[c, p].reshape(outputs, rows, modes_y)
            out_ref[p, c] = fold_rows(block, rows // high)


def pack_weights(layer, start, inputs, weights):
    _, parts, channels, _, modes_z, local_x, modes_y = weights.shape
    rows = modes_z * local_x
    fold = fold_count(rows, modes_y)
    packed = (rows // fold, fold * modes_y)
    return pl.pallas_call(
        functools.partial(pack_kernel, layer, start),
        in_specs=[pl.BlockSpec(memory_space=pl.ANY)],
        out_shape=jax.ShapeDtypeStruct((parts, inputs, channels, *packed), jnp.float32),
        scratch_shapes=[
            pltpu.VMEM((inputs, parts, channels, modes_z, local_x, modes_y), jnp.float32),
            pltpu.SemaphoreType.DMA((inputs, parts)),
        ],
        compiler_params=pltpu.CompilerParams(vmem_limit_bytes=28 << 20),
        cost_estimate=pl.CostEstimate(
            flops=0, bytes_accessed=5 * parts * inputs * channels * rows * LANES, transcendentals=0
        ),
        name="pack_weights",
    )(weights)


def y_kernel(count_y, *refs):
    data_refs, refs = refs[:count_y], refs[count_y:]
    *w_refs, f_ref, i_ref = refs[: -count_y - 2]
    out_refs, s_ref, m_ref = refs[-count_y - 2 : -2], refs[-2], refs[-1]
    inputs = [(w_ref, c) for w_ref in w_refs for c in range(w_ref.shape[1])]
    me = lax.axis_index("gy")
    modes_z, local_x, width = data_refs[0].shape
    groups = width // LANES
    rows = modes_z * local_x
    _, _, channels, high, wide = w_refs[0].shape
    fold = rows // high
    modes_y = wide // fold
    cg = channels // groups
    pair = 2 if count_y % 2 == 0 else 1

    full = None
    for first in range(0, count_y, pair):
        slots = range(first, first + pair)
        left = jnp.concatenate(
            [
                jnp.concatenate(
                    [
                        data_refs[s][:, :, g * LANES : (g + 1) * LANES].reshape(rows, LANES)
                        for g in range(groups)
                    ],
                    axis=0,
                )
                for s in slots
            ],
            axis=1,
        )
        right = [
            jnp.concatenate([f_ref[p, jnp.bitwise_xor(me, s)] for s in slots], axis=0)
            for p in range(2)
        ]
        term = dot3(split(left), right)
        full = term if full is None else full + term
    for g in range(groups):
        for c in range(cg):
            for q in range(2):
                start = (c * 2 + q) * modes_y
                block = full[g * rows : (g + 1) * rows, start : start + modes_y]
                s_ref[g * cg + c, q] = fold_rows(block, fold)

    for o in range(channels):
        real = imag = None
        for c, (w_ref, at) in enumerate(inputs):
            wr, wi = w_ref[0, at, o], w_ref[1, at, o]
            sr, si = s_ref[c, 0], s_ref[c, 1]
            a, b = wr * sr - wi * si, wr * si + wi * sr
            real, imag = (a, b) if c == 0 else (real + a, imag + b)
        m_ref[o, 0] = real
        m_ref[o, 1] = imag

    blocks = []
    for g in range(groups):
        for r in range(fold):
            pieces = [
                m_ref[g * cg + c, q][:, r * modes_y : (r + 1) * modes_y]
                for c in range(cg)
                for q in range(2)
            ]
            blocks.append(jnp.concatenate(pieces, axis=1))
    left = split(jnp.concatenate(blocks, axis=0))
    for first in range(0, count_y, pair):
        slots = range(first, first + pair)
        right = [
            jnp.concatenate([i_ref[p, jnp.bitwise_xor(me, s)] for s in slots], axis=1)
            for p in range(2)
        ]
        lines = dot3(left, right)
        for at, s in enumerate(slots):
            for g in range(groups):
                piece = lines[g * rows : (g + 1) * rows, at * LANES : (at + 1) * LANES]
                out_refs[s][:, :, g * LANES : (g + 1) * LANES] = piece.reshape(
                    modes_z, local_x, LANES
                )


def y_step(parts, weights, forward, inverse):
    count_y = len(parts)
    _, _, channels, high, wide = weights[0].shape
    shape = jax.ShapeDtypeStruct(parts[0].shape, jnp.float32)
    return pl.pallas_call(
        functools.partial(y_kernel, count_y),
        out_shape=[shape] * count_y,
        scratch_shapes=[pltpu.VMEM((channels, 2, high, wide), jnp.float32)] * 2,
        compiler_params=pltpu.CompilerParams(vmem_limit_bytes=14 << 20),
        name="y_step",
    )(*parts, *weights, forward, inverse)


def exchange(parts, axis):
    count = len(parts)
    moved = [parts[0]]
    for s in sorted(range(1, count), key=lambda s: (s < 2, s)):
        moved.append(lax.ppermute(parts[s], axis, [(i, i ^ s) for i in range(count)]))
    return [moved[0], moved[-1], *moved[1:-1]]


def constant_split(table):
    high = np.asarray(table, np.float32).astype(jnp.bfloat16)
    low = (np.asarray(table, np.float32) - high.astype(np.float32)).astype(jnp.bfloat16)
    return jnp.asarray(np.stack([high, low]))


def time_tables(rows_x, depth, total):
    cosine, sine = wave_tables(np.arange(MZ), depth)
    weight = np.where(np.arange(MZ) == 0, 1.0, 2.0)[:, None] / total
    forward = np.asarray(np.concatenate([cosine, -sine]).T, np.float32)
    high = forward.astype(jnp.bfloat16)
    low = (forward - high.astype(np.float32)).astype(jnp.bfloat16)
    first = np.arange(rows_x) < rows_x // 2
    forward = np.stack(
        [np.where(first, high[:, :, None], low[:, :, None]), np.repeat(high[:, :, None], rows_x, 2)]
    ).reshape(2, depth, -1)
    base = np.stack([cosine * weight, -sine * weight])
    high = np.asarray(base, np.float32).astype(jnp.bfloat16)
    low = (np.asarray(base, np.float32) - high.astype(np.float32)).astype(jnp.bfloat16)
    per = LANES // (4 * MZ)
    inverse = np.zeros((per, 2, per, 4, MZ, depth), high.dtype)
    for h in range(per):
        for part, value in enumerate((high, high, low)):
            inverse[h, :, h, part] = value
    return jnp.asarray(forward), jnp.asarray(inverse.reshape(per, 2 * LANES, depth))


def stack_columns(table):
    high = np.asarray(table, np.float32).astype(jnp.bfloat16)
    low = (np.asarray(table, np.float32) - high.astype(np.float32)).astype(jnp.bfloat16)
    return jnp.asarray(np.concatenate([high, low, high], axis=-1))


def x_tables(points_x, count_y):
    cosine, sine = wave_tables(mode_list(MX, points_x), points_x)
    both = np.stack([cosine.reshape(count_y, -1, points_x), sine.reshape(count_y, -1, points_x)], 1)
    forward = both.reshape(count_y, -1, points_x)
    return stack_columns(forward), stack_columns(np.concatenate([cosine.T, sine.T], 0))


def y_tables(points_y, rows_y):
    cosine, sine = wave_tables(mode_list(MY, points_y), points_y)
    count = points_y // rows_y
    cg = LANES // (2 * rows_y)
    cosine = cosine.reshape(MY, count, rows_y)
    sine = sine.reshape(MY, count, rows_y)
    fwd = np.stack([np.stack([cosine, -sine]), np.stack([sine, cosine])])
    inv = np.stack([np.stack([cosine, sine]), np.stack([-sine, cosine])])
    eye = np.eye(cg)
    fwd = np.einsum("ab,rqmgy->garybqm", eye, fwd).reshape(count, LANES, cg * 2 * MY)
    inv = np.einsum("ab,qrmgy->gaqmbry", eye, inv).reshape(count, cg * 2 * MY, LANES)
    return constant_split(fwd), constant_split(inv)


def shards(field, spectral_weight, point_weight, bias):
    channels, rows_x, rows_y, depth = field.shape
    layers = spectral_weight.shape[0]
    count_x = lax.axis_size("gx")
    count_y = lax.axis_size("gy")
    points_x = rows_x * count_x
    points_y = rows_y * count_y
    local_z = MZ // count_x
    fwd_z, inv_z = time_tables(rows_x, depth, float(points_x * points_y * depth))
    fwd_x, inv_x = x_tables(points_x, count_y)
    fwd_y, inv_y = y_tables(points_y, rows_y)
    half = channels // 2
    shares = ((0, half), (half, channels - half))

    def pack(layer, share):
        return pack_weights(layer, *shares[share], spectral_weight)

    current = field
    spectrum = first_step(
        pltpu.with_memory_space_constraint(field, pltpu.HBM),
        pltpu.with_memory_space_constraint(fwd_z, pltpu.HBM),
    )
    weights = []
    for layer in range(layers):
        data = spectrum.reshape(count_x, local_z, rows_x, -1)
        data = lax.all_to_all(data, "gx", 0, 0)
        parts = exchange(x_forward(rows_y, data, fwd_x), "gy")
        weights.append(pack(layer, 1) if weights else pack_weights(layer, 0, channels, spectral_weight))
        parts = exchange(y_step(parts, weights, fwd_y, inv_y), "gy")
        if layer + 1 < layers:
            parts, early = lax.optimization_barrier((parts, pack(layer + 1, 0)))
            weights = [early]
        data = x_inverse(rows_y, parts, inv_x, count_x)
        data = lax.all_to_all(data, "gx", 0, 0)
        planes = data.reshape(-1, LANES)
        if layer + 1 < layers:
            current, spectrum = time_step(layer, current, planes, inv_z, fwd_z, point_weight, bias)
        else:
            (current,) = time_step(layer, current, planes, inv_z, None, point_weight, bias)
    return current


def solution(mesh):
    return jax.shard_map(
        shards,
        mesh=mesh,
        in_specs=(P(None, "gx", "gy", None), P(None, None, None, None, "gx", "gy", None), P(), P()),
        out_specs=P(None, "gx", "gy", None),
        check_vma=False,
    )
```

```python
import functools

import jax
import jax.numpy as jnp
import numpy as np
from jax import lax
from jax.experimental import pallas as pl
from jax.experimental.pallas import tpu as pltpu
from jax.sharding import PartitionSpec as P

MZ = 16
MX = 64
MY = 32
LANES = 128
OCT = 8


def mode_list(count, points):
    half = count // 2
    lower = np.arange(half)
    return np.concatenate([lower, points - half + lower])


def wave_tables(modes, points):
    phase = 2.0 * np.pi / points * ((modes[:, None] * np.arange(points)[None, :]) % points)
    return np.cos(phase), np.sin(phase)


def split(value):
    high = value.astype(jnp.bfloat16)
    low = (value - high.astype(jnp.float32)).astype(jnp.bfloat16)
    return high, low


def whole_lanes(count):
    return -(-count // LANES) * LANES


def stack_rows(value):
    high, low = split(value)
    rows, columns = value.shape
    spare = whole_lanes(3 * rows) - 3 * rows
    pieces = [high, high, low]
    if spare:
        pieces.append(jnp.zeros((spare, columns), jnp.bfloat16))
    return jnp.concatenate(pieces, axis=0)


def dot3(left, right):
    def one(a, b):
        return jnp.dot(a, b, preferred_element_type=jnp.float32)

    return one(left[0], right[0]) + one(left[1], right[0]) + one(left[0], right[1])


def forward_rows(values, fwd_ref, rows_x):
    half = len(values)
    count = values[0].shape[0]
    high, low = split(jnp.concatenate(values, axis=0))
    one = jnp.dot(high, fwd_ref[0], preferred_element_type=jnp.float32)
    two = jnp.dot(low, fwd_ref[1], preferred_element_type=jnp.float32)
    lane = lax.broadcasted_iota(jnp.int32, (count, one.shape[1]), 1)
    picked = []
    for product in (one, two):
        total = product[:count]
        for i in range(1, half):
            here = product[i * count : (i + 1) * count]
            total = jnp.where(lane % half == i, here, total)
        picked.append(total)
    one, two = picked
    width = one.shape[1]
    other = jnp.where(
        lane % rows_x < half, pltpu.roll(one, width - half, axis=1), pltpu.roll(one, half, axis=1)
    )
    return one + other + two, lane % rows_x // half


def write_spectrum(acc, spec_ref, channels, rows_y):
    modes, local, width = spec_ref.shape
    n = modes * local
    cg = LANES // (2 * rows_y)
    for g in range(channels // cg):
        pieces = []
        for c in range(cg):
            for q in range(2):
                rows = slice((g * cg + c) * rows_y, (g * cg + c + 1) * rows_y)
                pieces.append(acc[rows, q * n : (q + 1) * n])
        turned = jnp.concatenate(pieces, axis=0).T
        spec_ref[:, :, g * LANES : (g + 1) * LANES] = turned.reshape(modes, local, LANES)


def first_kernel(u_ref, fwd_any, spec_ref, held, fwd_ref, acc, sems, table_sem):
    rows_x, channels, rows_y, depth = held.shape
    count = channels * rows_y
    table = pltpu.make_async_copy(fwd_any, fwd_ref, table_sem.at[0])

    def fetch(x):
        return pltpu.make_async_copy(u_ref.at[:, x], held.at[x], sems.at[x])

    table.start()
    for x in range(rows_x):
        fetch(x).start()
    table.wait()
    half = rows_x // 2
    for part in range(2):
        values = []
        for x in range(part * half, (part + 1) * half):
            fetch(x).wait()
            values.append(held[x].reshape(count, depth))
        term, owner = forward_rows(values, fwd_ref, rows_x)
        acc[...] = term if part == 0 else jnp.where(owner == part, term, acc[...])
    write_spectrum(acc, spec_ref, channels, rows_y)


def first_step(u, table):
    channels, rows_x, rows_y, depth = u.shape
    n = MZ * rows_x
    return pl.pallas_call(
        first_kernel,
        in_specs=[pl.BlockSpec(memory_space=pl.ANY)] * 2,
        out_shape=jax.ShapeDtypeStruct((MZ, rows_x, channels * 2 * rows_y), jnp.float32),
        scratch_shapes=[
            pltpu.VMEM((rows_x, channels, rows_y, depth), jnp.float32),
            pltpu.VMEM(table.shape, table.dtype),
            pltpu.VMEM((channels * rows_y, 2 * n), jnp.float32),
            pltpu.SemaphoreType.DMA((rows_x,)),
            pltpu.SemaphoreType.DMA((1,)),
        ],
        compiler_params=pltpu.CompilerParams(vmem_limit_bytes=14 << 20),
        name="first_step",
    )(u, table)


def pick_rows(channels):
    side = channels * OCT
    pick = lax.broadcasted_iota(jnp.int32, (side, channels), 0) // OCT
    return (pick == lax.broadcasted_iota(jnp.int32, (side, channels), 1)).astype(jnp.bfloat16)


def spread_rows(pick, part):
    return lax.dot_general(
        pick, part, (((1,), (1,)), ((), ())), preferred_element_type=jnp.float32
    )


def mix_table(layer, pick, point_ref, mix_ref):
    channels = point_ref.shape[1]
    side, wide = mix_ref.shape
    column = lax.broadcasted_iota(jnp.int32, (channels, wide), 1) % side // OCT
    place = column == lax.broadcasted_iota(jnp.int32, (channels, wide), 0)
    place = place.astype(jnp.bfloat16)
    column = lax.broadcasted_iota(jnp.int32, (side, wide), 1)
    same = lax.broadcasted_iota(jnp.int32, (side, wide), 0) % OCT == column % OCT
    full = []
    for part in split(point_ref[layer]):
        rows = spread_rows(pick, part).astype(jnp.bfloat16)
        full.append(jnp.dot(rows, place, preferred_element_type=jnp.float32))
    value = jnp.where((column >= side) & (column < 2 * side), full[1], full[0])
    mix_ref[...] = jnp.where(same, value, 0.0).astype(jnp.bfloat16)


def bias_table(layer, pick, bias_ref, wide_bias):
    channels = bias_ref.shape[1]
    lines = jnp.broadcast_to(bias_ref[layer : layer + 1, :], (LANES, channels))
    first = lines.astype(jnp.bfloat16)
    second, third = split(lines - first.astype(jnp.float32))
    wide_bias[...] = sum(spread_rows(pick, part) for part in (third, second, first))


def turn_planes(planes_ref, p_ref, channels, rows_y):
    cg = LANES // (2 * rows_y)
    groups = channels // cg
    rows_x = planes_ref.shape[0] // (MZ * groups)
    per = LANES // (4 * MZ)
    for pair in range(rows_x // per):
        for g in range(groups):
            pieces = []
            for x in range(pair * per, (pair + 1) * per):
                value = planes_ref[pl.ds(g * rows_x + x, MZ, stride=groups * rows_x), :]
                high = value.astype(jnp.bfloat16).astype(jnp.float32)
                pieces += [high, value - high, high, jnp.zeros_like(high)]
            turned = jnp.concatenate(pieces, axis=0).T.astype(jnp.bfloat16)
            for c in range(cg):
                for q in range(2):
                    src = slice((c * 2 + q) * rows_y, (c * 2 + q + 1) * rows_y)
                    dst = slice((g * cg + c) * rows_y, (g * cg + c + 1) * rows_y)
                    p_ref[pair, dst, q * LANES : (q + 1) * LANES] = turned[src]


def mix_rows(u_ref, i, rows, mixer):
    channels, _, _, depth = u_ref.shape
    x = u_ref[:, i, rows, :].reshape(channels * OCT, depth)
    high, low = split(x)
    right = jnp.concatenate([high, high, low], axis=0)
    return jnp.dot(mixer, right, preferred_element_type=jnp.float32)


def point_kernel(layer, u_ref, point_ref, out_ref, mix_ref):
    channels, rows_x, rows_y, depth = u_ref.shape
    mix_table(layer, pick_rows(channels), point_ref, mix_ref)
    mixer = mix_ref[...]
    for i in range(rows_x):
        for part in range(rows_y // OCT):
            rows = slice(part * OCT, (part + 1) * OCT)
            out_ref[:, i, rows, :] = mix_rows(u_ref, i, rows, mixer).reshape(channels, OCT, depth)


def point_step(layer, u, point_weight):
    channels = u.shape[0]
    side = channels * OCT
    return pl.pallas_call(
        functools.partial(point_kernel, layer),
        out_shape=jax.ShapeDtypeStruct(u.shape, jnp.float32),
        scratch_shapes=[pltpu.VMEM((side, 3 * side), jnp.bfloat16)],
        compiler_params=pltpu.CompilerParams(vmem_limit_bytes=14 << 20),
        cost_estimate=pl.CostEstimate(
            flops=6 * OCT * channels * u.size, bytes_accessed=8 * u.size, transcendentals=0
        ),
        name="point_step",
    )(u, point_weight)


def time_kernel(layer, has_forward, is_mixed, *refs):
    u_ref, planes_ref, inv_ref, bias_ref, *refs = refs
    if not is_mixed:
        point_ref, *refs = refs
    if has_forward:
        fwd_ref, out_ref, spec_ref, *refs, acc = refs
    else:
        out_ref, *refs = refs
    p_ref, wide_bias, *refs = refs
    if not is_mixed:
        (mix_ref,) = refs
    step = pl.program_id(0)
    channels, at_once, rows_y, depth = u_ref.shape
    rows_x = pl.num_programs(0) * at_once
    count = channels * rows_y
    per = inv_ref.shape[0]
    pairs = at_once // per

    @pl.when(step == 0)
    def _():
        turn_planes(planes_ref, p_ref, channels, rows_y)
        pick = pick_rows(channels)
        if not is_mixed:
            mix_table(layer, pick, point_ref, mix_ref)
        bias_table(layer, pick, bias_ref, wide_bias)

    left = jnp.concatenate([p_ref[step * pairs + i] for i in range(pairs)], axis=0)
    waves = [jnp.dot(left, inv_ref[h], preferred_element_type=jnp.float32) for h in range(per)]
    mixer = None if is_mixed else mix_ref[...]
    shift = jnp.concatenate([wide_bias[...]] * (depth // LANES), axis=1)
    for i in range(at_once):
        wave = waves[i % per][(i // per) * count : (i // per + 1) * count]
        wave = wave.reshape(channels, rows_y, depth)
        for part in range(rows_y // OCT):
            rows = slice(part * OCT, (part + 1) * OCT)
            x = u_ref[:, i, rows, :].reshape(channels * OCT, depth)
            local = x
            if not is_mixed:
                high, low = split(x)
                right = jnp.concatenate([high, high, low], axis=0)
                local = jnp.dot(mixer, right, preferred_element_type=jnp.float32)
            v = wave[:, rows, :].reshape(channels * OCT, depth) + local + shift
            v = v * (lax.erf(v * np.float32(np.sqrt(0.5))) + 1.0) * 0.5
            out_ref[:, i, rows, :] = v.reshape(channels, OCT, depth)

    if has_forward:
        values = [out_ref[:, i, :, :].reshape(count, depth) for i in range(at_once)]
        term, owner = forward_rows(values, fwd_ref, rows_x)

        @pl.when(step == 0)
        def _():
            acc[...] = term

        @pl.when(step == 1)
        def _():
            acc[...] = jnp.where(owner == 1, term, acc[...])

        @pl.when(step == pl.num_programs(0) - 1)
        def _():
            write_spectrum(acc, spec_ref, channels, rows_y)


def time_step(layer, u, planes, inverse, forward, bias, *pointwise):
    channels, rows_x, rows_y, depth = u.shape
    has_forward = forward is not None
    width = channels * 2 * rows_y
    n = MZ * rows_x
    side = channels * OCT
    per = inverse.shape[0]
    at_once = rows_x // 2
    block = pl.BlockSpec((channels, at_once, rows_y, depth), lambda s: (0, s, 0, 0))

    def whole(shape):
        return pl.BlockSpec(shape, lambda s: (0,) * len(shape))

    rest = [planes, inverse, bias, *pointwise] + ([forward] if has_forward else [])
    outs, out_specs = [jax.ShapeDtypeStruct(u.shape, jnp.float32)], [block]
    scratch = [
        pltpu.VMEM((rows_x // per, channels * rows_y, 2 * LANES), jnp.bfloat16),
        pltpu.VMEM((side, LANES), jnp.float32),
    ]
    if pointwise:
        scratch.append(pltpu.VMEM((side, 3 * side), jnp.bfloat16))
    if has_forward:
        outs.append(jax.ShapeDtypeStruct((MZ, rows_x, width), jnp.float32))
        out_specs.append(whole((MZ, rows_x, width)))
        scratch += [pltpu.VMEM((channels * rows_y, 2 * n), jnp.float32)]
    return pl.pallas_call(
        functools.partial(time_kernel, layer, has_forward, not pointwise),
        grid=(rows_x // at_once,),
        in_specs=[block] + [whole(a.shape) for a in rest],
        out_specs=out_specs,
        out_shape=outs,
        scratch_shapes=scratch,
        compiler_params=pltpu.CompilerParams(vmem_limit_bytes=14 << 20),
        name="time_step",
    )(u, *rest)


def turn(sign, rows_y, cosine, sine):
    lane = lax.broadcasted_iota(jnp.int32, cosine.shape, 1)
    ahead = pltpu.roll(sine, LANES - rows_y, axis=1)
    behind = pltpu.roll(sine, rows_y, axis=1)
    swapped = jnp.where((lane // rows_y) % 2 == 0, ahead, -behind)
    return cosine + swapped if sign > 0 else cosine - swapped


def x_forward_kernel(rows_y, data_ref, t_ref, *out_refs):
    me = lax.axis_index("gy")
    src, modes_z, per_src, width = data_ref.shape
    _, per_dst, _ = out_refs[0].shape
    table = jnp.concatenate([t_ref[jnp.bitwise_xor(me, s)] for s in range(len(out_refs))], axis=0)
    for k in range(modes_z):
        data = stack_rows(data_ref[:, k].reshape(src * per_src, width))
        both = jnp.dot(table, data, preferred_element_type=jnp.float32)
        for s, out_ref in enumerate(out_refs):
            top = 2 * s * per_dst
            for g in range(width // LANES):
                cols = slice(g * LANES, (g + 1) * LANES)
                cosine = both[top : top + per_dst, cols]
                sine = both[top + per_dst : top + 2 * per_dst, cols]
                out_ref[k, :, cols] = turn(1, rows_y, cosine, sine)


def x_forward(rows_y, data, table):
    src, modes_z, per_src, width = data.shape
    count_y, twice, _ = table.shape
    return pl.pallas_call(
        functools.partial(x_forward_kernel, rows_y),
        out_shape=[jax.ShapeDtypeStruct((modes_z, twice // 2, width), jnp.float32)] * count_y,
        compiler_params=pltpu.CompilerParams(vmem_limit_bytes=8 << 20),
        name="x_forward",
    )(data, table)


def x_inverse_kernel(rows_y, *refs):
    *data_refs, t_ref, out_ref, work = refs
    me = lax.axis_index("gy")
    for s, data_ref in enumerate(data_refs):
        work[jnp.bitwise_xor(me, s)] = data_ref[...]
    src, modes_z, per_src, width = work.shape
    dst, _, _, per_dst, _ = out_ref.shape
    n = dst * per_dst
    table = t_ref[...]
    for k in range(modes_z):
        data = stack_rows(work[:, k].reshape(src * per_src, width))
        both = jnp.dot(table, data, preferred_element_type=jnp.float32)
        for g in range(width // LANES):
            cols = slice(g * LANES, (g + 1) * LANES)
            value = turn(-1, rows_y, both[:n, cols], both[n:, cols])
            out_ref[:, k, g] = value.reshape(dst, per_dst, LANES)


def x_inverse(rows_y, parts, table, dst):
    modes_z, per_src, width = parts[0].shape
    per_dst = table.shape[0] // 2 // dst
    return pl.pallas_call(
        functools.partial(x_inverse_kernel, rows_y),
        out_shape=jax.ShapeDtypeStruct(
            (dst, modes_z, width // LANES, per_dst, LANES), jnp.float32
        ),
        scratch_shapes=[pltpu.VMEM((len(parts), modes_z, per_src, width), jnp.float32)],
        compiler_params=pltpu.CompilerParams(vmem_limit_bytes=8 << 20),
        name="x_inverse",
    )(*parts, table)


def fold_count(rows, modes_y):
    fold = max(1, LANES // modes_y)
    return fold if rows % (OCT * fold) == 0 else 1


def fold_rows(value, fold):
    step = value.shape[-2] // fold
    return jnp.concatenate(
        [value[..., r * step : (r + 1) * step, :] for r in range(fold)], axis=-1
    )


def pack_kernel(layer, start, w_ref, out_ref, held, sems):
    parts, inputs, outputs, high, _ = out_ref.shape
    modes_z, local_x, modes_y = held.shape[-3:]
    rows = modes_z * local_x

    def fetch(c, p):
        return pltpu.make_async_copy(
            w_ref.at[layer, p, start + c], held.at[c, p], sems.at[c, p]
        )

    @pl.loop(0, inputs)
    def _(c):
        for p in range(parts):
            fetch(c, p).start()

    @pl.loop(0, inputs)
    def _(c):
        for p in range(parts):
            fetch(c, p).wait()
            block = held[c, p].reshape(outputs, rows, modes_y)
            out_ref[p, c] = fold_rows(block, rows // high)


def pack_weights(layer, start, inputs, weights):
    _, parts, channels, _, modes_z, local_x, modes_y = weights.shape
    rows = modes_z * local_x
    fold = fold_count(rows, modes_y)
    packed = (rows // fold, fold * modes_y)
    return pl.pallas_call(
        functools.partial(pack_kernel, layer, start),
        in_specs=[pl.BlockSpec(memory_space=pl.ANY)],
        out_shape=jax.ShapeDtypeStruct((parts, inputs, channels, *packed), jnp.float32),
        scratch_shapes=[
            pltpu.VMEM((inputs, parts, channels, modes_z, local_x, modes_y), jnp.float32),
            pltpu.SemaphoreType.DMA((inputs, parts)),
        ],
        compiler_params=pltpu.CompilerParams(vmem_limit_bytes=28 << 20),
        cost_estimate=pl.CostEstimate(
            flops=0, bytes_accessed=5 * parts * inputs * channels * rows * LANES, transcendentals=0
        ),
        name="pack_weights",
    )(weights)


def y_kernel(count_y, *refs):
    data_refs, refs = refs[:count_y], refs[count_y:]
    *w_refs, f_ref, i_ref = refs[: -count_y - 2]
    out_refs, s_ref, m_ref = refs[-count_y - 2 : -2], refs[-2], refs[-1]
    inputs = [(w_ref, c) for w_ref in w_refs for c in range(w_ref.shape[1])]
    me = lax.axis_index("gy")
    modes_z, local_x, width = data_refs[0].shape
    groups = width // LANES
    rows = modes_z * local_x
    _, _, channels, high, wide = w_refs[0].shape
    fold = rows // high
    modes_y = wide // fold
    cg = channels // groups
    pair = 2 if count_y % 2 == 0 else 1

    full = None
    for first in range(0, count_y, pair):
        slots = range(first, first + pair)
        left = jnp.concatenate(
            [
                jnp.concatenate(
                    [
                        data_refs[s][:, :, g * LANES : (g + 1) * LANES].reshape(rows, LANES)
                        for g in range(groups)
                    ],
                    axis=0,
                )
                for s in slots
            ],
            axis=1,
        )
        right = [
            jnp.concatenate([f_ref[p, jnp.bitwise_xor(me, s)] for s in slots], axis=0)
            for p in range(2)
        ]
        term = dot3(split(left), right)
        full = term if full is None else full + term
    for g in range(groups):
        for c in range(cg):
            for q in range(2):
                start = (c * 2 + q) * modes_y
                block = full[g * rows : (g + 1) * rows, start : start + modes_y]
                s_ref[g * cg + c, q] = fold_rows(block, fold)

    for o in range(channels):
        real = imag = None
        for c, (w_ref, at) in enumerate(inputs):
            wr, wi = w_ref[0, at, o], w_ref[1, at, o]
            sr, si = s_ref[c, 0], s_ref[c, 1]
            a, b = wr * sr - wi * si, wr * si + wi * sr
            real, imag = (a, b) if c == 0 else (real + a, imag + b)
        m_ref[o, 0] = real
        m_ref[o, 1] = imag

    blocks = []
    for g in range(groups):
        for r in range(fold):
            pieces = [
                m_ref[g * cg + c, q][:, r * modes_y : (r + 1) * modes_y]
                for c in range(cg)
                for q in range(2)
            ]
            blocks.append(jnp.concatenate(pieces, axis=1))
    left = split(jnp.concatenate(blocks, axis=0))
    for first in range(0, count_y, pair):
        slots = range(first, first + pair)
        right = [
            jnp.concatenate([i_ref[p, jnp.bitwise_xor(me, s)] for s in slots], axis=1)
            for p in range(2)
        ]
        lines = dot3(left, right)
        for at, s in enumerate(slots):
            for g in range(groups):
                piece = lines[g * rows : (g + 1) * rows, at * LANES : (at + 1) * LANES]
                out_refs[s][:, :, g * LANES : (g + 1) * LANES] = piece.reshape(
                    modes_z, local_x, LANES
                )


def y_step(parts, weights, forward, inverse):
    count_y = len(parts)
    _, _, channels, high, wide = weights[0].shape
    shape = jax.ShapeDtypeStruct(parts[0].shape, jnp.float32)
    return pl.pallas_call(
        functools.partial(y_kernel, count_y),
        out_shape=[shape] * count_y,
        scratch_shapes=[pltpu.VMEM((channels, 2, high, wide), jnp.float32)] * 2,
        compiler_params=pltpu.CompilerParams(vmem_limit_bytes=14 << 20),
        name="y_step",
    )(*parts, *weights, forward, inverse)


def exchange(parts, axis):
    count = len(parts)
    moved = [parts[0]]
    for s in sorted(range(1, count), key=lambda s: (s < 2, s)):
        moved.append(lax.ppermute(parts[s], axis, [(i, i ^ s) for i in range(count)]))
    return [moved[0], moved[-1], *moved[1:-1]]


def constant_split(table):
    high = np.asarray(table, np.float32).astype(jnp.bfloat16)
    low = (np.asarray(table, np.float32) - high.astype(np.float32)).astype(jnp.bfloat16)
    return jnp.asarray(np.stack([high, low]))


def time_tables(rows_x, depth, total):
    cosine, sine = wave_tables(np.arange(MZ), depth)
    weight = np.where(np.arange(MZ) == 0, 1.0, 2.0)[:, None] / total
    forward = np.asarray(np.concatenate([cosine, -sine]).T, np.float32)
    high = forward.astype(jnp.bfloat16)
    low = (forward - high.astype(np.float32)).astype(jnp.bfloat16)
    first = np.arange(rows_x) < rows_x // 2
    forward = np.stack(
        [np.where(first, high[:, :, None], low[:, :, None]), np.repeat(high[:, :, None], rows_x, 2)]
    ).reshape(2, depth, -1)
    base = np.stack([cosine * weight, -sine * weight])
    high = np.asarray(base, np.float32).astype(jnp.bfloat16)
    low = (np.asarray(base, np.float32) - high.astype(np.float32)).astype(jnp.bfloat16)
    per = LANES // (4 * MZ)
    inverse = np.zeros((per, 2, per, 4, MZ, depth), high.dtype)
    for h in range(per):
        for part, value in enumerate((high, high, low)):
            inverse[h, :, h, part] = value
    return jnp.asarray(forward), jnp.asarray(inverse.reshape(per, 2 * LANES, depth))


def stack_columns(table):
    high = np.asarray(table, np.float32).astype(jnp.bfloat16)
    low = (np.asarray(table, np.float32) - high.astype(np.float32)).astype(jnp.bfloat16)
    stacked = np.concatenate([high, low, high], axis=-1)
    spare = whole_lanes(stacked.shape[-1]) - stacked.shape[-1]
    return jnp.asarray(np.pad(stacked, [(0, 0)] * (stacked.ndim - 1) + [(0, spare)]))


def x_tables(points_x, count_y):
    cosine, sine = wave_tables(mode_list(MX, points_x), points_x)
    both = np.stack([cosine.reshape(count_y, -1, points_x), sine.reshape(count_y, -1, points_x)], 1)
    forward = both.reshape(count_y, -1, points_x)
    return stack_columns(forward), stack_columns(np.concatenate([cosine.T, sine.T], 0))


def y_tables(points_y, rows_y):
    cosine, sine = wave_tables(mode_list(MY, points_y), points_y)
    count = points_y // rows_y
    cg = LANES // (2 * rows_y)
    cosine = cosine.reshape(MY, count, rows_y)
    sine = sine.reshape(MY, count, rows_y)
    fwd = np.stack([np.stack([cosine, -sine]), np.stack([sine, cosine])])
    inv = np.stack([np.stack([cosine, sine]), np.stack([-sine, cosine])])
    eye = np.eye(cg)
    fwd = np.einsum("ab,rqmgy->garybqm", eye, fwd).reshape(count, LANES, cg * 2 * MY)
    inv = np.einsum("ab,qrmgy->gaqmbry", eye, inv).reshape(count, cg * 2 * MY, LANES)
    return constant_split(fwd), constant_split(inv)


def shards(field, spectral_weight, point_weight, bias):
    channels, rows_x, rows_y, depth = field.shape
    layers = spectral_weight.shape[0]
    count_x = lax.axis_size("gx")
    count_y = lax.axis_size("gy")
    points_x = rows_x * count_x
    points_y = rows_y * count_y
    local_z = MZ // count_x
    fwd_z, inv_z = time_tables(rows_x, depth, float(points_x * points_y * depth))
    fwd_x, inv_x = x_tables(points_x, count_y)
    fwd_y, inv_y = y_tables(points_y, rows_y)
    half = channels // 2
    shares = ((0, half), (half, channels - half))

    def pack(layer, share):
        return pack_weights(layer, *shares[share], spectral_weight)

    current = field
    spectrum = first_step(
        pltpu.with_memory_space_constraint(field, pltpu.HBM),
        pltpu.with_memory_space_constraint(fwd_z, pltpu.HBM),
    )
    weights = []
    for layer in range(layers):
        data = spectrum.reshape(count_x, local_z, rows_x, -1)
        data = lax.all_to_all(data, "gx", 0, 0)
        parts = exchange(x_forward(rows_y, data, fwd_x), "gy")
        if weights:
            weights.append(pack(layer, 1))
        else:
            weights = [pack_weights(layer, 0, channels, spectral_weight)]
        parts = exchange(y_step(parts, weights, fwd_y, inv_y), "gy")
        if layer + 1 < layers:
            parts, ahead = lax.optimization_barrier((parts, pack(layer + 1, 0)))
            weights = [ahead]
        else:
            mixed = point_step(layer, current, point_weight)
            parts, mixed = lax.optimization_barrier((parts, mixed))
        data = x_inverse(rows_y, parts, inv_x, count_x)
        data = lax.all_to_all(data, "gx", 0, 0)
        planes = data.reshape(-1, LANES)
        if layer + 1 < layers:
            current, spectrum = time_step(layer, current, planes, inv_z, fwd_z, bias, point_weight)
        else:
            (current,) = time_step(layer, mixed, planes, inv_z, None, bias)
    return current


def solution(mesh):
    return jax.shard_map(
        shards,
        mesh=mesh,
        in_specs=(P(None, "gx", "gy", None), P(None, None, None, None, "gx", "gy", None), P(), P()),
        out_specs=P(None, "gx", "gy", None),
        check_vma=False,
    )
```
